256 devices in a mesh: section: 16 (over z, x_hi), dp: 16 (over y, x_lo, core).
Axes of the slice: x: 4 (x_hi: 2, x_lo: 2; x = x_hi * 2 + x_lo), y: 4, z: 8, core: 2. Of those that a mesh axis runs over, the one named last changes fastest.
Arguments:
- clip_pool: bfloat16 [64, 3, 4, 2, 640], P('dp'), may hold values from -6 to 6
- sample_ids: int32 [128], P('dp'), may hold values from 0 to 3
- timesteps: int32 [128], P('dp'), may hold values from 0 to 999
- noise_draw: bfloat16 [128, 3, 4, 2, 640], P('dp'), may hold values from -6 to 6
- keep_lists: int32 [128, 32], P('dp'), may hold values 0 or 1
- enc_weight: bfloat16 [16, 5760, 640], P('section'), may hold values from -0.078125 to 0.078125
- enc_gain: float32 [16, 640], P('section'), may hold values from 0.1 to 1.9
- dec_weight: bfloat16 [16, 1920, 640], P('section'), may hold values from -0.125 to 0.125
- dec_gain: float32 [16, 640], P('section'), may hold values from 0.1 to 1.9
Outputs:
- enc_weight_grad: float32 [16, 5760, 640], P('section', 'dp')
- enc_gain_grad: float32 [16, 640], P('section', 'dp')
- dec_weight_grad: float32 [16, 1920, 640], P('section', 'dp')
- dec_gain_grad: float32 [16, 640], P('section', 'dp')
The draws below stay inside these ranges and needn't reach their ends.
All inputs are finite; a program needn't handle non-finite values. No bound on the sum of `keep_lists` on one device may be relied on, other than what follows from the above.
Results may differ from the reference program's by a relative error of at most 0.025.
Values may be sent and summed in bfloat16 or wider, within the bound.
A program may use at most 64 MiB of HBM per device.

```python
import math
import jax
import jax.numpy as jnp
from jax import lax

CHANNELS = 640
GROUPS = 32
FRAMES = 3
HEIGHT = 4
WIDTH = 2
MICRO = 8
POOL_DEV = 4
LEVELS = 16
SAMPLES = 128
POOL = 64


def touch_ends(result, rng, least, top_value):
    longest = result.shape.index(max(result.shape))
    spots = []
    for shift in (0, 1):
        where = [jax.random.randint(jax.random.fold_in(rng, axis), (), 0, length) for axis, length in enumerate(result.shape)]
        where[longest] = (where[longest] + shift) % result.shape[longest]
        spots.append(tuple(where))
    return result.at[spots[0]].set(least).at[spots[1]].set(top_value)


def levels(own_key, extent, split, least, largest):
    gain = 1.0
    for dim, blocks in split:
        heights = jax.random.uniform(jax.random.fold_in(jax.random.fold_in(own_key, 6), dim), (blocks,), jnp.float32, least / len(split), largest / len(split))
        gain = gain * jnp.repeat(jnp.exp(heights), extent[dim] // blocks).reshape((-1,) + (1,) * (len(extent) - 1 - dim))
    return gain


def gaussian(key, shape, deviation, most, split=(), kind=jnp.bfloat16):
    loudness = levels(key, shape, split, -0.22, 0.18) if split else 1.0
    drawn = jax.random.normal(key, shape, jnp.float32) * deviation * loudness
    return jnp.minimum(jnp.maximum(drawn, -most), most).astype(kind)


def setup_inputs(seed: int = 0) -> dict:
    key_of = jax.random.split(jax.random.key(seed), 10)
    clip_pool = gaussian(key_of[0], (POOL, FRAMES, HEIGHT, WIDTH, CHANNELS), 1.0, 6.0, ((0, 16),))
    sample_ids = touch_ends(jax.random.randint(key_of[1], (SAMPLES,), 0, POOL_DEV), jax.random.fold_in(key_of[1], 1), 0, POOL_DEV - 1).astype(jnp.int32)
    timesteps = touch_ends(jax.random.randint(key_of[2], (SAMPLES,), 0, 1000), jax.random.fold_in(key_of[2], 1), 0, 999).astype(jnp.int32)
    noise_draw = gaussian(key_of[3], (SAMPLES, FRAMES, HEIGHT, WIDTH, CHANNELS), 1.0, 6.0, ((0, 16),))
    keep_lists = touch_ends((jax.random.randint(key_of[4], (SAMPLES, 2 * LEVELS), 0, 4) < 3).astype(jnp.int32), jax.random.fold_in(key_of[4], 1), 0, 1)
    enc_weight = gaussian(key_of[5], (LEVELS, 9 * CHANNELS, CHANNELS), (9 * CHANNELS) ** -0.5, 0.078125, ((0, 16),))
    enc_gain = jnp.clip(1.0 + 0.18 * jax.random.normal(key_of[6], (LEVELS, CHANNELS), jnp.float32), 0.1, 1.9)
    dec_weight = gaussian(key_of[7], (LEVELS, 3 * CHANNELS, CHANNELS), (3 * CHANNELS) ** -0.5, 0.125, ((0, 16),))
    dec_gain = jnp.clip(1.0 + 0.18 * jax.random.normal(key_of[8], (LEVELS, CHANNELS), jnp.float32), 0.1, 1.9)
    return dict(clip_pool=clip_pool, sample_ids=sample_ids, timesteps=timesteps, noise_draw=noise_draw, keep_lists=keep_lists, enc_weight=enc_weight, enc_gain=enc_gain, dec_weight=dec_weight, dec_gain=dec_gain)


def noise_level(timesteps):
    phase_arg = (timesteps.astype(jnp.float32) / 1000.0 + 0.008) / 1.008
    return jnp.cos(phase_arg * (math.pi / 2.0)) ** 2

def norm_act(values, gain_rows):
    batch_size = values.shape[0]
    channels = values.shape[-1]
    grouped = values.reshape(batch_size, -1, GROUPS, channels // GROUPS)
    center = grouped - lax.optimization_barrier(jnp.mean(grouped, axis=(1, 3), keepdims=True))
    spread = lax.optimization_barrier(jnp.mean(center * center, axis=(1, 3), keepdims=True))
    normed = (center * lax.rsqrt(spread + 1e-05)).reshape(values.shape)
    return jax.nn.silu(normed * gain_rows[:, None, None, None, :])

def spatial_columns(activation):
    grid_height = activation.shape[2]
    grid_width = activation.shape[3]
    padded = jnp.pad(activation, ((0, 0), (0, 0), (1, 1), (1, 1), (0, 0)))
    pieces = [padded[:, :, row_shift:row_shift + grid_height, col_shift:col_shift + grid_width, :] for row_shift in range(3) for col_shift in range(3)]
    return jnp.concatenate(pieces, axis=-1).reshape(-1, 9 * activation.shape[-1])

def spatial_spread(columns, full_shape):
    batch_size, frames, grid_height, grid_width, channels = full_shape
    columns = columns.reshape(batch_size, frames, grid_height, grid_width, 9, channels)
    summed = jnp.zeros((batch_size, frames, grid_height + 2, grid_width + 2, channels), jnp.float32)
    for kernel_tap in range(9):
        row_shift = kernel_tap // 3
        col_shift = kernel_tap % 3
        summed = summed + jnp.pad(columns[:, :, :, :, kernel_tap, :], ((0, 0), (0, 0), (row_shift, 2 - row_shift), (col_shift, 2 - col_shift), (0, 0)))
    return summed[:, :, 1:grid_height + 1, 1:grid_width + 1, :]

def temporal_columns(activation):
    frames = activation.shape[1]
    padded = jnp.pad(activation, ((0, 0), (1, 1), (0, 0), (0, 0), (0, 0)))
    pieces = [padded[:, frame_shift:frame_shift + frames] for frame_shift in range(3)]
    return jnp.concatenate(pieces, axis=-1).reshape(-1, 3 * activation.shape[-1])

def temporal_spread(columns, full_shape):
    batch_size, frames, grid_height, grid_width, channels = full_shape
    columns = columns.reshape(batch_size, frames, grid_height, grid_width, 3, channels)
    summed = jnp.zeros((batch_size, frames + 2, grid_height, grid_width, channels), jnp.float32)
    for kernel_tap in range(3):
        summed = summed + jnp.pad(columns[:, :, :, :, kernel_tap, :], ((0, 0), (kernel_tap, 2 - kernel_tap), (0, 0), (0, 0), (0, 0)))
    return summed[:, 1:frames + 1]

def gate_shape(keep_rate):
    return keep_rate[:, None, None, None, None]

def encoder_forward(stream, weight, gain_rows, keep_rate):
    activation = norm_act(stream.astype(jnp.float32), gain_rows).astype(jnp.bfloat16)
    branch = jnp.dot(spatial_columns(activation), weight, preferred_element_type=jnp.float32)
    return (stream.astype(jnp.float32) + gate_shape(keep_rate) * branch.reshape(stream.shape)).astype(jnp.bfloat16)

def encoder_backward(stream, upstream, weight, gain_rows, keep_rate):
    activation, pullback = jax.vjp(norm_act, stream.astype(jnp.float32), gain_rows)
    columns = spatial_columns(activation.astype(jnp.bfloat16))
    gated = (gate_shape(keep_rate) * upstream.astype(jnp.float32)).astype(jnp.bfloat16).reshape(-1, stream.shape[-1])
    back_cols = lax.dot_general(gated, weight, (((1,), (1,)), ((), ())), preferred_element_type=jnp.float32)
    norm_grad, gain_grad = pullback(spatial_spread(back_cols, stream.shape))
    stream_grad = (upstream.astype(jnp.float32) + norm_grad).astype(jnp.bfloat16)
    return (stream_grad, columns, gated, gain_grad)

def decoder_forward(stream, skip_act, weight, gain_rows, keep_rate):
    merged = stream.astype(jnp.float32) + skip_act.astype(jnp.float32)
    activation = norm_act(merged, gain_rows).astype(jnp.bfloat16)
    branch = jnp.dot(temporal_columns(activation), weight, preferred_element_type=jnp.float32)
    return (stream.astype(jnp.float32) + gate_shape(keep_rate) * branch.reshape(stream.shape)).astype(jnp.bfloat16)

def decoder_backward(stream, skip_act, upstream, weight, gain_rows, keep_rate):
    merged = stream.astype(jnp.float32) + skip_act.astype(jnp.float32)
    activation, pullback = jax.vjp(norm_act, merged, gain_rows)
    columns = temporal_columns(activation.astype(jnp.bfloat16))
    gated = (gate_shape(keep_rate) * upstream.astype(jnp.float32)).astype(jnp.bfloat16).reshape(-1, stream.shape[-1])
    back_cols = lax.dot_general(gated, weight, (((1,), (1,)), ((), ())), preferred_element_type=jnp.float32)
    merged_grad, gain_grad = pullback(temporal_spread(back_cols, stream.shape))
    stream_grad = (upstream.astype(jnp.float32) + merged_grad).astype(jnp.bfloat16)
    return (stream_grad, merged_grad.astype(jnp.bfloat16), columns, gated, gain_grad)

def group_total(terms):
    grouped = terms.reshape((SAMPLES // MICRO, MICRO) + terms.shape[1:]).sum(axis=1)
    rounded = lax.optimization_barrier(grouped.astype(jnp.bfloat16))
    return lax.optimization_barrier(jnp.sum(rounded.astype(jnp.float32), axis=0))

def weight_total(columns, gated):
    group_count = SAMPLES // MICRO
    left_rows = columns.reshape(group_count, -1, columns.shape[-1]).astype(jnp.float32)
    right_rows = gated.reshape(group_count, -1, gated.shape[-1]).astype(jnp.float32)
    per_group = jnp.einsum('gtk,gtc->gkc', left_rows, right_rows, precision=lax.Precision.HIGHEST)
    rounded = lax.optimization_barrier(per_group.astype(jnp.bfloat16))
    return lax.optimization_barrier(jnp.sum(rounded.astype(jnp.float32), axis=0))

def reference(clip_pool, sample_ids, timesteps, noise_draw, keep_lists, enc_weight, enc_gain, dec_weight, dec_gain):
    owners = jnp.arange(SAMPLES, dtype=jnp.int32) // MICRO * POOL_DEV + sample_ids.astype(jnp.int32)
    clean = jnp.take(clip_pool, owners, axis=0).astype(jnp.float32)
    level_noise = noise_level(timesteps)[:, None, None, None, None]
    stream = (jnp.sqrt(level_noise) * clean + jnp.sqrt(1.0 - level_noise) * noise_draw.astype(jnp.float32)).astype(jnp.bfloat16)
    keep_rates = keep_lists.astype(jnp.float32)
    enc_inputs = []
    skip_acts = []
    for level_index in range(LEVELS):
        gain_rows = jnp.broadcast_to(enc_gain[level_index], (SAMPLES, CHANNELS))
        enc_inputs.append(stream)
        stream = encoder_forward(stream, enc_weight[level_index], gain_rows, keep_rates[:, level_index])
        skip_acts.append(stream)
    dec_inputs = []
    for level_index in range(LEVELS):
        gain_rows = jnp.broadcast_to(dec_gain[level_index], (SAMPLES, CHANNELS))
        dec_inputs.append(stream)
        stream = decoder_forward(stream, skip_acts[LEVELS - 1 - level_index], dec_weight[level_index], gain_rows, keep_rates[:, LEVELS + level_index])
    scale = 1.0 / math.sqrt(SAMPLES * FRAMES * HEIGHT * WIDTH)
    upstream = ((stream.astype(jnp.float32) - noise_draw.astype(jnp.float32)) * scale).astype(jnp.bfloat16)
    dec_weight_terms = [None] * LEVELS
    dec_gain_terms = [None] * LEVELS
    skip_grads = [None] * LEVELS
    for level_index in reversed(range(LEVELS)):
        gain_rows = jnp.broadcast_to(dec_gain[level_index], (SAMPLES, CHANNELS))
        stream_grad, skip_grad, columns, gated, gain_grad = decoder_backward(dec_inputs[level_index], skip_acts[LEVELS - 1 - level_index], upstream, dec_weight[level_index], gain_rows, keep_rates[:, LEVELS + level_index])
        dec_weight_terms[level_index] = weight_total(columns, gated)
        dec_gain_terms[level_index] = group_total(gain_grad)
        skip_grads[LEVELS - 1 - level_index] = skip_grad
        upstream = stream_grad
    enc_weight_terms = [None] * LEVELS
    enc_gain_terms = [None] * LEVELS
    for level_index in reversed(range(LEVELS)):
        gain_rows = jnp.broadcast_to(enc_gain[level_index], (SAMPLES, CHANNELS))
        summed_grad = (upstream.astype(jnp.float32) + skip_grads[level_index].astype(jnp.float32)).astype(jnp.bfloat16)
        stream_grad, columns, gated, gain_grad = encoder_backward(enc_inputs[level_index], summed_grad, enc_weight[level_index], gain_rows, keep_rates[:, level_index])
        enc_weight_terms[level_index] = weight_total(columns, gated)
        enc_gain_terms[level_index] = group_total(gain_grad)
        upstream = stream_grad
    return (jnp.stack(enc_weight_terms), jnp.stack(enc_gain_terms), jnp.stack(dec_weight_terms), jnp.stack(dec_gain_terms))
```

```python
import math

import jax
import jax.numpy as jnp
import numpy as np
from jax import lax
from jax.experimental import pallas as pl
from jax.experimental.pallas import tpu as pltpu
from jax.sharding import PartitionSpec as P

GROUPS = 32
F32, BF16 = jnp.float32, jnp.bfloat16
MESH = pl.DeviceIdType.MESH
PACE = 2


def noise_level(timesteps):
    phase_arg = (timesteps.astype(F32) / 1000.0 + 0.008) / 1.008
    return jnp.cos(phase_arg * (math.pi / 2.0)) ** 2


def over_rows(values):
    part = values[0] + values[1] + values[2]
    return jnp.broadcast_to(jnp.sum(part, axis=0, keepdims=True), part.shape)


def split_terms(values):
    high = values.astype(BF16).astype(F32)
    rest = values - high
    middle = rest.astype(BF16).astype(F32)
    return [high, middle, rest - middle]


def group_means(rows, mix_ref, count):
    terms = [term for row in rows for term in split_terms(row)]
    stacked = jnp.concatenate(terms, axis=0).astype(BF16)
    sums = jnp.dot(stacked, mix_ref[...], preferred_element_type=F32)
    return [
        (sums[24 * i : 24 * i + 8] + sums[24 * i + 8 : 24 * i + 16] + sums[24 * i + 16 : 24 * i + 24])
        * (1.0 / count)
        for i in range(len(rows))
    ]


def cube(values):
    return values.reshape(3, 8, values.shape[-1])


def padded_rows(values):
    full = jnp.concatenate([values, jnp.zeros((1,) + values.shape[1:], F32)], axis=0)
    return full.reshape(32, values.shape[-1]).astype(BF16)


def spatial_taps(values, sign):
    place = lax.broadcasted_iota(jnp.int32, values.shape, 1)
    high, wide = place // 2, place % 2
    taps = []
    for tap in range(9):
        down, across = sign * (tap // 3 - 1), sign * (tap % 3 - 1)
        shift = 2 * down + across
        moved = pltpu.roll(values, (-shift) % 8, 1) if shift % 8 else values
        if down or across:
            inside = (
                (high + down >= 0) & (high + down < 4) & (wide + across >= 0) & (wide + across < 2)
            )
            moved = jnp.where(inside, moved, 0.0)
        taps.append(padded_rows(moved))
    return taps


def temporal_taps(values, sign):
    zero = jnp.zeros_like(values[:1])
    before = jnp.concatenate([zero, values[:2]], axis=0)
    after = jnp.concatenate([values[1:], zero], axis=0)
    taps = [before, values, after] if sign > 0 else [after, values, before]
    return [padded_rows(tap) for tap in taps]


def norm_forward(values, gain, mix_ref, count):
    mean = group_means([over_rows(values)], mix_ref, count)[0]
    center = values - mean[None]
    spread = group_means([over_rows(center * center)], mix_ref, count)[0]
    scale = lax.rsqrt(spread + 1e-05)
    normed = center * scale[None]
    z = normed * gain[None]
    gate = 1.0 / (1.0 + jnp.exp(-z))
    return normed, scale, z, gate


def norm_backward(cot, normed, scale, slope, gain, mix_ref, count):
    dz = cot * slope
    gain_part = dz * normed
    gain_part = gain_part[0] + gain_part[1] + gain_part[2]
    dn = dz * gain[None]
    mean_dn, mean_dnn = group_means([over_rows(dn), over_rows(dn * normed)], mix_ref, count)
    return scale[None] * (dn - mean_dn[None] - normed * mean_dnn[None]), gain_part


def transposed_product(taps, weight_ref, channels):
    total = None
    for index, tap in enumerate(taps):
        part = lax.dot_general(
            tap,
            weight_ref[pl.ds(index * channels, channels), :],
            (((1,), (1,)), ((), ())),
            preferred_element_type=F32,
        )
        total = part if total is None else total + part
    return total


def pipeline_kernel(
    sections,
    micros,
    loss_scale,
    keep_ref,
    first_ref,
    noise_ref,
    enc_gain_ref,
    dec_gain_ref,
    mix_ref,
    enc_hbm,
    dec_hbm,
    dwe_ref,
    dwd_ref,
    dge_ref,
    dgd_ref,
    enc_w,
    dec_w,
    fwd_in,
    bwd_in,
    skip_in,
    scot_in,
    enc_out,
    dec_out,
    g_out,
    s_out,
    q_out,
    enc_normed,
    dec_normed,
    enc_slope,
    dec_slope,
    enc_scale,
    dec_scale,
    enc_act,
    dec_act,
    enc_cot,
    dec_cot,
    turned,
    local_sem,
    fwd_sem,
    bwd_sem,
    skip_sem,
    scot_sem,
    send_sem,
):
    channels = noise_ref.shape[-1]
    count = 24 * (channels // GROUPS)
    own = lax.axis_index("section")
    last = sections - 1
    after = lax.rem(own + 1, sections)
    before = lax.rem(own + last, sections)
    mirror = last - own
    wrap_up = (own + 1) // sections
    wrap_down = (last - own) // last

    load_enc = pltpu.make_async_copy(enc_hbm, enc_w, local_sem.at[0])
    load_dec = pltpu.make_async_copy(dec_hbm, dec_w, local_sem.at[1])
    load_enc.start()
    load_dec.start()

    barrier = pltpu.get_barrier_semaphore()
    for other in (after, before, mirror):
        pl.semaphore_signal(barrier, inc=1, device_id={"section": other}, device_id_type=MESH)
    pl.semaphore_wait(barrier, 3)

    @pl.when(own == 0)
    def _():
        for j in range(micros):
            fwd_in[j] = first_ref[j]

    dge_ref[...] = jnp.zeros_like(dge_ref)
    dgd_ref[...] = jnp.zeros_like(dgd_ref)
    load_enc.wait()
    load_dec.wait()

    def send(source, j, target, slot, arrive, kind, other):
        return pltpu.make_async_remote_copy(
            src_ref=source.at[j],
            dst_ref=target.at[slot],
            send_sem=send_sem.at[kind, j],
            recv_sem=arrive.at[slot],
            device_id={"section": other},
            device_id_type=MESH,
        )

    def arrived(buffer, slot, sem):
        pltpu.make_async_copy(buffer.at[slot], buffer.at[slot], sem.at[slot]).wait()

    def turn(source):
        turned[...] = source[...].astype(F32).T.astype(BF16)

    def step(t, carry):
        def window(start):
            j = t - start
            return j, (j >= 0) & (j < micros)

        j_ef, enc_fwd = window(own * PACE)

        @pl.when(enc_fwd)
        def _():
            j = j_ef

            @pl.when(own > 0)
            def _():
                arrived(fwd_in, j, fwd_sem)

            values = cube(fwd_in[j].astype(F32))
            keep = keep_ref[j, own].astype(F32)
            gain = enc_gain_ref[...]
            normed, scale, z, gate = norm_forward(values, gain, mix_ref, count)
            act = z * gate
            columns = jnp.concatenate(spatial_taps(act, 1), axis=1)
            branch = jnp.dot(columns, enc_w[...], preferred_element_type=F32)
            result = values + keep * cube(branch[:24])
            enc_out[j] = result.reshape(24, channels).astype(BF16)
            send(enc_out, j, fwd_in, j + micros * wrap_up, fwd_sem, 0, after).start()
            send(enc_out, j, skip_in, j, skip_sem, 1, mirror).start()
            enc_normed[j] = normed
            enc_scale[j] = scale
            enc_slope[j] = gate * (1.0 + z * (1.0 - gate))
            enc_act[pl.ds(pl.multiple_of(j * 32, 32), 32), :] = padded_rows(act)

        j_df, dec_fwd = window((sections + own) * PACE)

        @pl.when(dec_fwd)
        def _():
            j = j_df
            arrived(fwd_in, micros + j, fwd_sem)
            arrived(skip_in, j, skip_sem)
            stream = cube(fwd_in[micros + j].astype(F32))
            values = stream + cube(skip_in[j].astype(F32))
            keep = keep_ref[j, sections + own].astype(F32)
            gain = dec_gain_ref[...]
            normed, scale, z, gate = norm_forward(values, gain, mix_ref, count)
            act = z * gate
            columns = jnp.concatenate(temporal_taps(act, 1), axis=1)
            branch = jnp.dot(columns, dec_w[...], preferred_element_type=F32)
            result = (stream + keep * cube(branch[:24])).reshape(24, channels).astype(BF16)
            dec_out[j] = result

            @pl.when(own < last)
            def _():
                send(dec_out, j, fwd_in, micros + j, fwd_sem, 2, after).start()

            @pl.when(own == last)
            def _():
                gap = result.astype(F32) - noise_ref[j].astype(F32)
                bwd_in[j] = (gap * loss_scale).astype(BF16)

            dec_normed[j] = normed
            dec_scale[j] = scale
            dec_slope[j] = gate * (1.0 + z * (1.0 - gate))
            dec_act[pl.ds(pl.multiple_of(j * 32, 32), 32), :] = padded_rows(act)

        j_db, dec_bwd = window((3 * sections - 2 - own) * PACE)

        @pl.when(dec_bwd)
        def _():
            j = j_db

            @pl.when(own < last)
            def _():
                arrived(bwd_in, j, bwd_sem)

            upstream = cube(bwd_in[j].astype(F32))
            keep = keep_ref[j, sections + own].astype(F32)
            taps = temporal_taps(keep * upstream, -1)
            cot = cube(transposed_product(taps, dec_w, channels)[:24])
            grad, gain_part = norm_backward(
                cot, dec_normed[j], dec_scale[j], dec_slope[j], dec_gain_ref[...], mix_ref, count
            )
            g_out[j] = (upstream + grad).reshape(24, channels).astype(BF16)
            send(g_out, j, bwd_in, j + micros * wrap_down, bwd_sem, 3, before).start()
            s_out[j] = grad.reshape(24, channels).astype(BF16)
            send(s_out, j, scot_in, j, scot_sem, 4, mirror).start()
            dgd_ref[...] += gain_part
            dec_cot[pl.ds(pl.multiple_of(j * 32, 32), 32), :] = jnp.concatenate(taps, axis=1)

        @pl.when(t == (3 * sections - 2 - own) * PACE + micros)
        def _():
            turn(dec_act)
            for tap in range(3):
                dwd_ref[tap * channels : (tap + 1) * channels, :] = jnp.dot(
                    turned[...],
                    dec_cot[:, tap * channels : (tap + 1) * channels],
                    preferred_element_type=F32,
                ).astype(BF16)
            turn(enc_act)

        j_eb, enc_bwd = window((4 * sections - 2 - own) * PACE)

        @pl.when(enc_bwd)
        def _():
            j = j_eb
            arrived(scot_in, j, scot_sem)
            arrived(bwd_in, micros + j, bwd_sem)
            upstream = fwd_sum(bwd_in[micros + j], scot_in[j])
            keep = keep_ref[j, own].astype(F32)
            taps = spatial_taps(keep * upstream, -1)
            cot = cube(transposed_product(taps, enc_w, channels)[:24])
            grad, gain_part = norm_backward(
                cot, enc_normed[j], enc_scale[j], enc_slope[j], enc_gain_ref[...], mix_ref, count
            )

            @pl.when(own > 0)
            def _():
                q_out[j] = (upstream + grad).reshape(24, channels).astype(BF16)
                send(q_out, j, bwd_in, micros + j, bwd_sem, 5, before).start()

            dge_ref[...] += gain_part
            enc_cot[pl.ds(pl.multiple_of(j * 32, 32), 32), :] = jnp.concatenate(taps, axis=1)

        return carry

    def fwd_sum(stream, skip):
        return cube((stream.astype(F32) + skip.astype(F32)).astype(BF16).astype(F32))

    lax.fori_loop(0, (4 * sections - 2) * PACE + micros, step, 0)
    for tap in range(9):
        dwe_ref[tap * channels : (tap + 1) * channels, :] = jnp.dot(
            turned[...],
            enc_cot[:, tap * channels : (tap + 1) * channels],
            preferred_element_type=F32,
        ).astype(BF16)

    def drain(j, carry):
        for kind, source in ((0, enc_out), (1, enc_out), (3, g_out), (4, s_out)):
            pltpu.make_async_copy(source.at[j], source.at[j], send_sem.at[kind, j]).wait()

        @pl.when(own < last)
        def _():
            pltpu.make_async_copy(dec_out.at[j], dec_out.at[j], send_sem.at[2, j]).wait()

        @pl.when(own > 0)
        def _():
            pltpu.make_async_copy(q_out.at[j], q_out.at[j], send_sem.at[5, j]).wait()

        return carry

    lax.fori_loop(0, micros, drain, 0)


def body(
    clip_pool,
    sample_ids,
    timesteps,
    noise_draw,
    keep_lists,
    enc_weight,
    enc_gain,
    dec_weight,
    dec_gain,
):
    sections = lax.axis_size("section")
    micros = noise_draw.shape[0]
    channels = noise_draw.shape[-1]
    positions = noise_draw.shape[1] * noise_draw.shape[2] * noise_draw.shape[3]
    scale = 1.0 / math.sqrt(micros * lax.axis_size("dp") * positions)
    flat = (micros, positions, channels)
    noise = noise_draw.reshape(flat)
    clips = clip_pool.reshape((-1,) + flat[1:])
    clean = jnp.zeros(flat, F32)
    for clip in range(clips.shape[0]):
        clean = jnp.where((sample_ids == clip)[:, None, None], clips[clip][None].astype(F32), clean)
    level = noise_level(timesteps)[:, None, None]
    first = (jnp.sqrt(level) * clean + jnp.sqrt(1.0 - level) * noise.astype(F32)).astype(BF16)
    member = np.arange(channels) // (channels // GROUPS)
    mix = jnp.asarray((member[:, None] == member[None, :]).astype(np.float32), BF16)
    vmem = pl.BlockSpec(memory_space=pltpu.VMEM)
    hbm = pl.BlockSpec(memory_space=pl.ANY)
    slots = lambda n: pltpu.VMEM((n, positions, channels), BF16)
    kept = lambda: pltpu.VMEM((micros, 3, 8, channels), F32)
    rows = 32 * micros
    dwe, dwd, dge, dgd = pl.pallas_call(
        lambda *refs: pipeline_kernel(sections, micros, scale, *refs),
        out_shape=(
            jax.ShapeDtypeStruct((9 * channels, channels), BF16),
            jax.ShapeDtypeStruct((3 * channels, channels), BF16),
            jax.ShapeDtypeStruct((8, channels), F32),
            jax.ShapeDtypeStruct((8, channels), F32),
        ),
        in_specs=[pl.BlockSpec(memory_space=pltpu.SMEM), vmem, vmem, vmem, vmem, vmem, hbm, hbm],
        out_specs=(vmem, vmem, vmem, vmem),
        scratch_shapes=[
            pltpu.VMEM((9 * channels, channels), BF16),
            pltpu.VMEM((3 * channels, channels), BF16),
            slots(2 * micros),
            slots(2 * micros),
            slots(micros),
            slots(micros),
            slots(micros),
            slots(micros),
            slots(micros),
            slots(micros),
            slots(micros),
            kept(),
            kept(),
            kept(),
            kept(),
            pltpu.VMEM((micros, 8, channels), F32),
            pltpu.VMEM((micros, 8, channels), F32),
            pltpu.VMEM((rows, channels), BF16),
            pltpu.VMEM((rows, channels), BF16),
            pltpu.VMEM((rows, 9 * channels), BF16),
            pltpu.VMEM((rows, 3 * channels), BF16),
            pltpu.VMEM((channels, rows), BF16),
            pltpu.SemaphoreType.DMA((2,)),
            pltpu.SemaphoreType.DMA((2 * micros,)),
            pltpu.SemaphoreType.DMA((2 * micros,)),
            pltpu.SemaphoreType.DMA((micros,)),
            pltpu.SemaphoreType.DMA((micros,)),
            pltpu.SemaphoreType.DMA((6, micros)),
        ],
        compiler_params=pltpu.CompilerParams(
            collective_id=0, has_side_effects=True, vmem_limit_bytes=56 << 20
        ),
        name="pipeline",
    )(keep_lists, first, noise, enc_gain, dec_gain, mix, enc_weight[0], dec_weight[0])
    gains = jnp.stack([jnp.sum(dge, axis=0), jnp.sum(dgd, axis=0)]).astype(BF16)
    scatter = lambda value, dim: lax.psum_scatter(
        value, "dp", scatter_dimension=dim, tiled=True
    ).astype(F32)
    dwe, dwd, gains = scatter(dwe, 0), scatter(dwd, 0), scatter(gains, 1)
    return (dwe[None], gains[:1], dwd[None], gains[1:])


def solution(mesh):
    placed = (
        P("dp", None, None, None, None),
        P("dp"),
        P("dp"),
        P("dp", None, None, None, None),
        P("dp", None),
        P("section", None, None),
        P("section", None),
        P("section", None, None),
        P("section", None),
    )
    return jax.shard_map(
        body,
        mesh=mesh,
        in_specs=placed,
        out_specs=(
            P("section", "dp", None),
            P("section", "dp"),
            P("section", "dp", None),
            P("section", "dp"),
        ),
        check_vma=False,
    )
```

```python
import math

import jax
import jax.numpy as jnp
import numpy as np
from jax import lax
from jax.experimental import pallas as pl
from jax.experimental.pallas import tpu as pltpu
from jax.sharding import PartitionSpec as P

GROUPS = 32
F32, BF16 = jnp.float32, jnp.bfloat16
MESH = pl.DeviceIdType.MESH
PACE = 2


def noise_level(timesteps):
    phase_arg = (timesteps.astype(F32) / 1000.0 + 0.008) / 1.008
    return jnp.cos(phase_arg * (math.pi / 2.0)) ** 2


def over_rows(values):
    part = values[0] + values[1] + values[2]
    return jnp.broadcast_to(jnp.sum(part, axis=0, keepdims=True), part.shape)


def split_terms(values):
    high = values.astype(BF16).astype(F32)
    rest = values - high
    middle = rest.astype(BF16).astype(F32)
    return [high, middle, rest - middle]


def group_means(rows, mix_ref, count):
    terms = [term for row in rows for term in split_terms(row)]
    stacked = jnp.concatenate(terms, axis=0).astype(BF16)
    sums = jnp.dot(stacked, mix_ref[...], preferred_element_type=F32)
    return [
        (sums[24 * i : 24 * i + 8] + sums[24 * i + 8 : 24 * i + 16] + sums[24 * i + 16 : 24 * i + 24])
        * (1.0 / count)
        for i in range(len(rows))
    ]


def cube(values):
    return values.reshape(3, 8, values.shape[-1])


def padded_rows(values):
    full = jnp.concatenate([values, jnp.zeros((1,) + values.shape[1:], F32)], axis=0)
    return full.reshape(32, values.shape[-1]).astype(BF16)


def spatial_taps(values, sign):
    place = lax.broadcasted_iota(jnp.int32, values.shape, 1)
    high, wide = place // 2, place % 2
    taps = []
    for tap in range(9):
        down, across = sign * (tap // 3 - 1), sign * (tap % 3 - 1)
        shift = 2 * down + across
        moved = pltpu.roll(values, (-shift) % 8, 1) if shift % 8 else values
        if down or across:
            inside = (
                (high + down >= 0) & (high + down < 4) & (wide + across >= 0) & (wide + across < 2)
            )
            moved = jnp.where(inside, moved, 0.0)
        taps.append(padded_rows(moved))
    return taps


def temporal_taps(values, sign):
    zero = jnp.zeros_like(values[:1])
    before = jnp.concatenate([zero, values[:2]], axis=0)
    after = jnp.concatenate([values[1:], zero], axis=0)
    taps = [before, values, after] if sign > 0 else [after, values, before]
    return [padded_rows(tap) for tap in taps]


def norm_forward(values, gain, mix_ref, count):
    mean = group_means([over_rows(values)], mix_ref, count)[0]
    center = values - mean[None]
    spread = group_means([over_rows(center * center)], mix_ref, count)[0]
    scale = lax.rsqrt(spread + 1e-05)
    normed = center * scale[None]
    z = normed * gain[None]
    gate = 1.0 / (1.0 + jnp.exp(-z))
    return normed, scale, z, gate


def norm_backward(cot, normed, scale, slope, gain, mix_ref, count):
    dz = cot * slope
    gain_part = dz * normed
    gain_part = gain_part[0] + gain_part[1] + gain_part[2]
    dn = dz * gain[None]
    mean_dn, mean_dnn = group_means([over_rows(dn), over_rows(dn * normed)], mix_ref, count)
    return scale[None] * (dn - mean_dn[None] - normed * mean_dnn[None]), gain_part


def scatter_start(p, c, sibling, dw, from_sibling, pair, from_chips, sems):
    chips = dw.shape[0]
    send_pair, arrive_pair, send_chip, arrive_chip = sems

    def to_sibling(o, carry):
        m = lax.rem(p + o, chips)
        pltpu.make_async_remote_copy(
            src_ref=dw.at[m, 1 - c],
            dst_ref=from_sibling.at[m],
            send_sem=send_pair.at[m],
            recv_sem=arrive_pair.at[m],
            device_id={"dp": sibling},
            device_id_type=MESH,
        ).start()
        return carry

    def to_chip(o, carry):
        m = lax.rem(p + o, chips)
        pltpu.make_async_copy(from_sibling.at[m], from_sibling.at[m], arrive_pair.at[m]).wait()

        def add(block, inner):
            pair[m, block] = (
                dw[m, c, block].astype(F32) + from_sibling[m, block].astype(F32)
            ).astype(BF16)
            return inner

        lax.fori_loop(0, dw.shape[2], add, 0)
        pltpu.make_async_remote_copy(
            src_ref=pair.at[m],
            dst_ref=from_chips.at[o - 1],
            send_sem=send_chip.at[o - 1],
            recv_sem=arrive_chip.at[o - 1],
            device_id={"dp": 2 * m + c},
            device_id_type=MESH,
        ).start()
        return carry

    lax.fori_loop(1, chips + 1, to_sibling, 0)
    lax.fori_loop(1, chips, to_chip, 0)
    pltpu.make_async_copy(from_sibling.at[p], from_sibling.at[p], arrive_pair.at[p]).wait()


def scatter_end(p, c, dw, from_sibling, pair, from_chips, sems, out_ref):
    chips = dw.shape[0]
    send_pair, arrive_pair, send_chip, arrive_chip = sems

    def arrive(o, carry):
        pltpu.make_async_copy(from_chips.at[o], from_chips.at[o], arrive_chip.at[o]).wait()
        return carry

    def add(block, carry):
        total = dw[p, c, block].astype(F32) + from_sibling[p, block].astype(F32)
        for o in range(chips - 1):
            total = total + from_chips[o, block].astype(F32)
        out_ref[block] = total
        return carry

    def sent(o, carry):
        pltpu.make_async_copy(pair.at[o], pair.at[o], send_chip.at[o]).wait()
        return carry

    def sent_pair(m, carry):
        pltpu.make_async_copy(from_sibling.at[m], from_sibling.at[m], send_pair.at[m]).wait()
        return carry

    lax.fori_loop(0, chips - 1, arrive, 0)
    lax.fori_loop(0, dw.shape[2], add, 0)
    lax.fori_loop(0, chips - 1, sent, 0)
    lax.fori_loop(0, chips, sent_pair, 0)


def weight_terms(turned, cot, dw, channels):
    blocks = dw.shape[2]
    for tap in range(cot.shape[1] // channels):
        part = jnp.dot(
            turned[...],
            cot[:, tap * channels : (tap + 1) * channels],
            preferred_element_type=F32,
        ).reshape(channels // 40, 40, channels)
        for i in range(channels // 40):
            at = tap * (channels // 40) + i
            dw[at // (2 * blocks), (at // blocks) % 2, at % blocks] = part[i].astype(BF16)


def pipeline_kernel(
    sections,
    micros,
    loss_scale,
    keep_ref,
    first_ref,
    noise_ref,
    enc_gain_ref,
    dec_gain_ref,
    mix_ref,
    enc_hbm,
    dec_hbm,
    dwe_out,
    dwd_out,
    gain_out,
    enc_w,
    dec_w,
    dec_wt,
    fwd_in,
    bwd_in,
    skip_in,
    scot_in,
    enc_out,
    dec_out,
    g_out,
    s_out,
    q_out,
    enc_normed,
    dec_normed,
    enc_slope,
    dec_slope,
    enc_scale,
    dec_scale,
    enc_act,
    dec_act,
    enc_cot,
    dec_cot,
    turned,
    dge_ref,
    dgd_ref,
    gain_own,
    gain_pair,
    gain_sibling,
    gain_chips,
    enc_dw,
    enc_sibling,
    enc_pair,
    enc_chips,
    dec_dw,
    dec_sibling,
    dec_pair,
    dec_chips,
    local_sem,
    fwd_sem,
    bwd_sem,
    skip_sem,
    scot_sem,
    send_sem,
    enc_pair_sem,
    enc_chip_sem,
    dec_pair_sem,
    dec_chip_sem,
    gain_pair_sem,
    gain_chip_sem,
):
    channels = noise_ref.shape[-1]
    count = 24 * (channels // GROUPS)
    own = lax.axis_index("section")
    last = sections - 1
    after = lax.rem(own + 1, sections)
    before = lax.rem(own + last, sections)
    mirror = last - own
    wrap_up = (own + 1) // sections
    wrap_down = (last - own) // last

    load_enc = pltpu.make_async_copy(enc_hbm, enc_w, local_sem.at[0])
    load_dec = pltpu.make_async_copy(dec_hbm, dec_w, local_sem.at[1])
    load_enc.start()
    load_dec.start()

    dp = lax.axis_index("dp")
    p, c = dp // 2, lax.rem(dp, 2)
    sibling = dp + 1 - 2 * c
    chips = enc_dw.shape[0]
    enc_sems = [enc_pair_sem.at[0], enc_pair_sem.at[1], enc_chip_sem.at[0], enc_chip_sem.at[1]]
    dec_sems = [dec_pair_sem.at[0], dec_pair_sem.at[1], dec_chip_sem.at[0], dec_chip_sem.at[1]]

    barrier = pltpu.get_barrier_semaphore()
    for other in (after, before, mirror):
        pl.semaphore_signal(barrier, inc=1, device_id={"section": other}, device_id_type=MESH)
    pl.semaphore_signal(barrier, inc=1, device_id={"dp": sibling}, device_id_type=MESH)
    for o in range(1, chips):
        pl.semaphore_signal(
            barrier,
            inc=1,
            device_id={"dp": 2 * lax.rem(p + o, chips) + c},
            device_id_type=MESH,
        )
    pl.semaphore_wait(barrier, 3 + chips)

    @pl.when(own == 0)
    def _():
        for j in range(micros):
            fwd_in[j] = first_ref[j]

    dge_ref[...] = jnp.zeros_like(dge_ref)
    dgd_ref[...] = jnp.zeros_like(dgd_ref)
    load_enc.wait()
    load_dec.wait()

    def send(source, j, target, slot, arrive, kind, other):
        return pltpu.make_async_remote_copy(
            src_ref=source.at[j],
            dst_ref=target.at[slot],
            send_sem=send_sem.at[kind, j],
            recv_sem=arrive.at[slot],
            device_id={"section": other},
            device_id_type=MESH,
        )

    def arrived(buffer, slot, sem):
        pltpu.make_async_copy(buffer.at[slot], buffer.at[slot], sem.at[slot]).wait()

    def turn(source):
        turned[...] = source[...].astype(F32).T.astype(BF16)

    def step(t, carry):
        def window(start):
            j = t - start
            return j, (j >= 0) & (j < micros)

        j_ef, enc_fwd = window(own * PACE)

        @pl.when(enc_fwd)
        def _():
            j = j_ef

            @pl.when(own > 0)
            def _():
                arrived(fwd_in, j, fwd_sem)

            values = cube(fwd_in[j].astype(F32))
            keep = keep_ref[j, own].astype(F32)
            gain = enc_gain_ref[...]
            normed, scale, z, gate = norm_forward(values, gain, mix_ref, count)
            act = z * gate
            columns = jnp.concatenate(spatial_taps(act, 1), axis=1)
            branch = jnp.dot(columns, enc_w[...], preferred_element_type=F32)
            result = values + keep * cube(branch[:24])
            enc_out[j] = result.reshape(24, channels).astype(BF16)
            send(enc_out, j, fwd_in, j + micros * wrap_up, fwd_sem, 0, after).start()
            send(enc_out, j, skip_in, j, skip_sem, 1, mirror).start()
            enc_normed[j] = normed
            enc_scale[j] = scale
            enc_slope[j] = gate * (1.0 + z * (1.0 - gate))
            enc_act[pl.ds(pl.multiple_of(j * 32, 32), 32), :] = padded_rows(act)

        @pl.when(t == own * PACE + micros)
        def _():
            def tap_enc(tap, inner):
                rows = pl.ds(pl.multiple_of(tap * channels, channels), channels)
                enc_w[rows, :] = enc_w[rows, :].astype(F32).T.astype(BF16)
                return inner

            def tap_dec(tap, inner):
                rows = pl.ds(pl.multiple_of(tap * channels, channels), channels)
                dec_wt[rows, :] = dec_w[rows, :].astype(F32).T.astype(BF16)
                return inner

            lax.fori_loop(0, 9, tap_enc, 0)
            lax.fori_loop(0, 3, tap_dec, 0)

        j_df, dec_fwd = window((sections + own) * PACE)

        @pl.when(dec_fwd)
        def _():
            j = j_df
            arrived(fwd_in, micros + j, fwd_sem)
            arrived(skip_in, j, skip_sem)
            stream = cube(fwd_in[micros + j].astype(F32))
            values = stream + cube(skip_in[j].astype(F32))
            keep = keep_ref[j, sections + own].astype(F32)
            gain = dec_gain_ref[...]
            normed, scale, z, gate = norm_forward(values, gain, mix_ref, count)
            act = z * gate
            columns = jnp.concatenate(temporal_taps(act, 1), axis=1)
            branch = jnp.dot(columns, dec_w[...], preferred_element_type=F32)
            result = (stream + keep * cube(branch[:24])).reshape(24, channels).astype(BF16)
            dec_out[j] = result

            @pl.when(own < last)
            def _():
                send(dec_out, j, fwd_in, micros + j, fwd_sem, 2, after).start()

            @pl.when(own == last)
            def _():
                gap = result.astype(F32) - noise_ref[j].astype(F32)
                bwd_in[j] = (gap * loss_scale).astype(BF16)

            dec_normed[j] = normed
            dec_scale[j] = scale
            dec_slope[j] = gate * (1.0 + z * (1.0 - gate))
            dec_act[pl.ds(pl.multiple_of(j * 32, 32), 32), :] = padded_rows(act)

        j_db, dec_bwd = window((3 * sections - 2 - own) * PACE)

        @pl.when(dec_bwd)
        def _():
            j = j_db

            @pl.when(own < last)
            def _():
                arrived(bwd_in, j, bwd_sem)

            upstream = cube(bwd_in[j].astype(F32))
            keep = keep_ref[j, sections + own].astype(F32)
            taps = temporal_taps(keep * upstream, -1)
            columns = jnp.concatenate(taps, axis=1)
            cot = cube(jnp.dot(columns, dec_wt[...], preferred_element_type=F32)[:24])
            grad, gain_part = norm_backward(
                cot, dec_normed[j], dec_scale[j], dec_slope[j], dec_gain_ref[...], mix_ref, count
            )
            g_out[j] = (upstream + grad).reshape(24, channels).astype(BF16)
            send(g_out, j, bwd_in, j + micros * wrap_down, bwd_sem, 3, before).start()
            s_out[j] = grad.reshape(24, channels).astype(BF16)
            send(s_out, j, scot_in, j, scot_sem, 4, mirror).start()
            dgd_ref[...] += gain_part
            dec_cot[pl.ds(pl.multiple_of(j * 32, 32), 32), :] = columns

        @pl.when(t == (3 * sections - 2 - own) * PACE + micros)
        def _():
            turn(dec_act)
            weight_terms(turned, dec_cot, dec_dw, channels)
            turn(enc_act)
            scatter_start(p, c, sibling, dec_dw, dec_sibling, dec_pair, dec_chips, dec_sems)

        j_eb, enc_bwd = window((4 * sections - 2 - own) * PACE)

        @pl.when(enc_bwd)
        def _():
            j = j_eb
            arrived(scot_in, j, scot_sem)
            arrived(bwd_in, micros + j, bwd_sem)
            upstream = fwd_sum(bwd_in[micros + j], scot_in[j])
            keep = keep_ref[j, own].astype(F32)
            taps = spatial_taps(keep * upstream, -1)
            columns = jnp.concatenate(taps, axis=1)
            cot = cube(jnp.dot(columns, enc_w[...], preferred_element_type=F32)[:24])
            grad, gain_part = norm_backward(
                cot, enc_normed[j], enc_scale[j], enc_slope[j], enc_gain_ref[...], mix_ref, count
            )

            @pl.when(own > 0)
            def _():
                q_out[j] = (upstream + grad).reshape(24, channels).astype(BF16)
                send(q_out, j, bwd_in, micros + j, bwd_sem, 5, before).start()

            dge_ref[...] += gain_part
            enc_cot[pl.ds(pl.multiple_of(j * 32, 32), 32), :] = columns

        return carry

    def fwd_sum(stream, skip):
        return cube((stream.astype(F32) + skip.astype(F32)).astype(BF16).astype(F32))

    lax.fori_loop(0, (4 * sections - 2) * PACE + micros, step, 0)
    row = lax.broadcasted_iota(jnp.int32, (8, channels), 0)
    gain_own[...] = jnp.where(
        row == 0,
        jnp.sum(dge_ref[...], axis=0, keepdims=True),
        jnp.where(row == 1, jnp.sum(dgd_ref[...], axis=0, keepdims=True), 0.0),
    )
    to_pair = pltpu.make_async_remote_copy(
        src_ref=gain_own,
        dst_ref=gain_sibling,
        send_sem=gain_pair_sem.at[0],
        recv_sem=gain_pair_sem.at[1],
        device_id={"dp": sibling},
        device_id_type=MESH,
    )
    to_pair.start()
    weight_terms(turned, enc_cot, enc_dw, channels)
    scatter_start(p, c, sibling, enc_dw, enc_sibling, enc_pair, enc_chips, enc_sems)
    to_pair.wait()
    gain_pair[...] = gain_own[...] + gain_sibling[...]

    def gain_to_chip(o, carry):
        pltpu.make_async_remote_copy(
            src_ref=gain_pair,
            dst_ref=gain_chips.at[o - 1],
            send_sem=gain_chip_sem.at[0, o - 1],
            recv_sem=gain_chip_sem.at[1, o - 1],
            device_id={"dp": 2 * lax.rem(p + o, chips) + c},
            device_id_type=MESH,
        ).start()
        return carry

    lax.fori_loop(1, chips, gain_to_chip, 0)
    scatter_end(p, c, dec_dw, dec_sibling, dec_pair, dec_chips, dec_sems, dwd_out)
    scatter_end(p, c, enc_dw, enc_sibling, enc_pair, enc_chips, enc_sems, dwe_out)

    def gain_arrived(o, carry):
        for side in range(2):
            pltpu.make_async_copy(
                gain_chips.at[o], gain_chips.at[o], gain_chip_sem.at[side, o]
            ).wait()
        return carry

    lax.fori_loop(0, chips - 1, gain_arrived, 0)
    total = gain_pair[...]
    for o in range(chips - 1):
        total = total + gain_chips[o]
    gain_out[...] = total

    def drain(j, carry):
        for kind, source in ((0, enc_out), (1, enc_out), (3, g_out), (4, s_out)):
            pltpu.make_async_copy(source.at[j], source.at[j], send_sem.at[kind, j]).wait()

        @pl.when(own < last)
        def _():
            pltpu.make_async_copy(dec_out.at[j], dec_out.at[j], send_sem.at[2, j]).wait()

        @pl.when(own > 0)
        def _():
            pltpu.make_async_copy(q_out.at[j], q_out.at[j], send_sem.at[5, j]).wait()

        return carry

    lax.fori_loop(0, micros, drain, 0)


def body(
    clip_pool,
    sample_ids,
    timesteps,
    noise_draw,
    keep_lists,
    enc_weight,
    enc_gain,
    dec_weight,
    dec_gain,
):
    sections = lax.axis_size("section")
    micros = noise_draw.shape[0]
    channels = noise_draw.shape[-1]
    positions = noise_draw.shape[1] * noise_draw.shape[2] * noise_draw.shape[3]
    scale = 1.0 / math.sqrt(micros * lax.axis_size("dp") * positions)
    flat = (micros, positions, channels)
    noise = noise_draw.reshape(flat)
    clips = clip_pool.reshape((-1,) + flat[1:])
    clean = jnp.zeros(flat, F32)
    for clip in range(clips.shape[0]):
        clean = jnp.where((sample_ids == clip)[:, None, None], clips[clip][None].astype(F32), clean)
    level = noise_level(timesteps)[:, None, None]
    first = (jnp.sqrt(level) * clean + jnp.sqrt(1.0 - level) * noise.astype(F32)).astype(BF16)
    member = np.arange(channels) // (channels // GROUPS)
    mix = jnp.asarray((member[:, None] == member[None, :]).astype(np.float32), BF16)
    vmem = pl.BlockSpec(memory_space=pltpu.VMEM)
    hbm = pl.BlockSpec(memory_space=pl.ANY)
    slots = lambda n: pltpu.VMEM((n, positions, channels), BF16)
    kept = lambda: pltpu.VMEM((micros, 3, 8, channels), F32)
    rows = 32 * micros
    group = lax.axis_size("dp")
    chips = group // 2
    wide = lambda *lead: pltpu.VMEM(lead + (40, channels), BF16)
    enc_blocks, dec_blocks = 9 * channels // group // 40, 3 * channels // group // 40
    shares = lambda n: [wide(chips, 2, n), wide(chips, n), wide(chips, n), wide(chips - 1, n)]
    dwe, dwd, gains = pl.pallas_call(
        lambda *refs: pipeline_kernel(sections, micros, scale, *refs),
        out_shape=(
            jax.ShapeDtypeStruct((enc_blocks, 40, channels), F32),
            jax.ShapeDtypeStruct((dec_blocks, 40, channels), F32),
            jax.ShapeDtypeStruct((8, channels), F32),
        ),
        in_specs=[pl.BlockSpec(memory_space=pltpu.SMEM), vmem, vmem, vmem, vmem, vmem, hbm, hbm],
        out_specs=(vmem, vmem, vmem),
        scratch_shapes=[
            pltpu.VMEM((9 * channels, channels), BF16),
            pltpu.VMEM((3 * channels, channels), BF16),
            pltpu.VMEM((3 * channels, channels), BF16),
            slots(2 * micros),
            slots(2 * micros),
            slots(micros),
            slots(micros),
            slots(micros),
            slots(micros),
            slots(micros),
            slots(micros),
            slots(micros),
            kept(),
            kept(),
            kept(),
            kept(),
            pltpu.VMEM((micros, 8, channels), F32),
            pltpu.VMEM((micros, 8, channels), F32),
            pltpu.VMEM((rows, channels), BF16),
            pltpu.VMEM((rows, channels), BF16),
            pltpu.VMEM((rows, 9 * channels), BF16),
            pltpu.VMEM((rows, 3 * channels), BF16),
            pltpu.VMEM((channels, rows), BF16),
            pltpu.VMEM((8, channels), F32),
            pltpu.VMEM((8, channels), F32),
            pltpu.VMEM((8, channels), F32),
            pltpu.VMEM((8, channels), F32),
            pltpu.VMEM((8, channels), F32),
            pltpu.VMEM((chips - 1, 8, channels), F32),
            *shares(enc_blocks),
            *shares(dec_blocks),
            pltpu.SemaphoreType.DMA((2,)),
            pltpu.SemaphoreType.DMA((2 * micros,)),
            pltpu.SemaphoreType.DMA((2 * micros,)),
            pltpu.SemaphoreType.DMA((micros,)),
            pltpu.SemaphoreType.DMA((micros,)),
            pltpu.SemaphoreType.DMA((6, micros)),
            pltpu.SemaphoreType.DMA((2, chips)),
            pltpu.SemaphoreType.DMA((2, chips - 1)),
            pltpu.SemaphoreType.DMA((2, chips)),
            pltpu.SemaphoreType.DMA((2, chips - 1)),
            pltpu.SemaphoreType.DMA((2,)),
            pltpu.SemaphoreType.DMA((2, chips - 1)),
        ],
        compiler_params=pltpu.CompilerParams(
            collective_id=0, has_side_effects=True, vmem_limit_bytes=60 << 20
        ),
        name="pipeline",
    )(keep_lists, first, noise, enc_gain, dec_gain, mix, enc_weight[0], dec_weight[0])
    part = channels // group
    gains = lax.dynamic_slice_in_dim(gains, lax.axis_index("dp") * part, part, 1)
    return (
        dwe.reshape(1, -1, channels),
        gains[0:1],
        dwd.reshape(1, -1, channels),
        gains[1:2],
    )


def solution(mesh):
    placed = (
        P("dp", None, None, None, None),
        P("dp"),
        P("dp"),
        P("dp", None, None, None, None),
        P("dp", None),
        P("section", None, None),
        P("section", None),
        P("section", None, None),
        P("section", None),
    )
    return jax.shard_map(
        body,
        mesh=mesh,
        in_specs=placed,
        out_specs=(
            P("section", "dp", None),
            P("section", "dp"),
            P("section", "dp", None),
            P("section", "dp"),
        ),
        check_vma=False,
    )
```

```python
import math

import jax
import jax.numpy as jnp
import numpy as np
from jax import lax
from jax.experimental import pallas as pl
from jax.experimental.pallas import tpu as pltpu
from jax.sharding import PartitionSpec as P

GROUPS = 32
F32, BF16 = jnp.float32, jnp.bfloat16
MESH = pl.DeviceIdType.MESH


def noise_level(timesteps):
    phase_arg = (timesteps.astype(F32) / 1000.0 + 0.008) / 1.008
    return jnp.cos(phase_arg * (math.pi / 2.0)) ** 2


def over_rows(values):
    part = values[:, 0] + values[:, 1] + values[:, 2]
    return jnp.broadcast_to(jnp.sum(part, axis=1, keepdims=True), part.shape)


def split_terms(values):
    high = values.astype(BF16).astype(F32)
    rest = values - high
    middle = rest.astype(BF16).astype(F32)
    return [high, middle, rest - middle]


def group_means(sums, mix_ref, count):
    terms = [term for each in sums for term in split_terms(each)]
    stacked = jnp.concatenate(terms, axis=0)
    samples, rows, channels = sums[0].shape
    mixed = jnp.dot(
        stacked.reshape(-1, channels).astype(BF16), mix_ref[...], preferred_element_type=F32
    ).reshape(-1, samples, rows, channels)
    return [
        (mixed[3 * i] + mixed[3 * i + 1] + mixed[3 * i + 2]) * (1.0 / count)
        for i in range(len(sums))
    ]


def cube(values):
    return values.reshape(-1, 3, 8, values.shape[-1])


def uncube(product):
    return product.reshape(-1, 4, 8, product.shape[-1])[:, :3]


def flat(values):
    return values.reshape(-1, 24, values.shape[-1]).astype(BF16)


def padded_rows(values):
    full = jnp.concatenate([values, jnp.zeros_like(values[:, :1])], axis=1)
    return full.reshape(-1, values.shape[-1]).astype(BF16)


def spatial_taps(values, sign):
    place = lax.broadcasted_iota(jnp.int32, values.shape, 2)
    high, wide = place // 2, place % 2
    taps = []
    for tap in range(9):
        down, across = sign * (tap // 3 - 1), sign * (tap % 3 - 1)
        shift = 2 * down + across
        moved = pltpu.roll(values, (-shift) % 8, 2) if shift % 8 else values
        if down or across:
            inside = (
                (high + down >= 0) & (high + down < 4) & (wide + across >= 0) & (wide + across < 2)
            )
            moved = jnp.where(inside, moved, 0.0)
        taps.append(padded_rows(moved))
    return jnp.concatenate(taps, axis=1)


def temporal_taps(values, sign):
    zero = jnp.zeros_like(values[:, :1])
    before = jnp.concatenate([zero, values[:, :2]], axis=1)
    after = jnp.concatenate([values[:, 1:], zero], axis=1)
    taps = [before, values, after] if sign > 0 else [after, values, before]
    return jnp.concatenate([padded_rows(tap) for tap in taps], axis=1)


def norm_forward(values, gain, mix_ref, count):
    mean = group_means([over_rows(values)], mix_ref, count)[0]
    center = values - mean[:, None]
    spread = group_means([over_rows(center * center)], mix_ref, count)[0]
    scale = lax.rsqrt(spread + 1e-05)
    normed = center * scale[:, None]
    z = normed * gain[None, None]
    gate = 1.0 / (1.0 + jnp.exp(-z))
    return normed, scale, z, gate


def norm_backward(cot, normed, scale, slope, gain, mix_ref, count):
    dz = cot * slope
    gain_part = dz * normed
    gain_part = jnp.sum(gain_part[:, 0] + gain_part[:, 1] + gain_part[:, 2], axis=0)
    dn = dz * gain[None, None]
    mean_dn, mean_dnn = group_means([over_rows(dn), over_rows(dn * normed)], mix_ref, count)
    grad = scale[:, None] * (dn - mean_dn[:, None] - normed * mean_dnn[:, None])
    return grad, gain_part


def gated(values, keeps):
    return jnp.concatenate([values[s : s + 1] * keep for s, keep in enumerate(keeps)], axis=0)


def transposed_product(columns, weight_ref, channels):
    total = None
    for at in range(0, columns.shape[1], channels):
        part = lax.dot_general(
            columns[:, at : at + channels],
            weight_ref[at : at + channels, :],
            (((1,), (1,)), ((), ())),
            preferred_element_type=F32,
        )
        total = part if total is None else total + part
    return total


def scatter_start(p, c, sibling, dw, from_sibling, pair, from_chips, sems):
    chips = dw.shape[0]
    send_pair, arrive_pair, send_chip, arrive_chip = sems

    def to_sibling(o, carry):
        m = lax.rem(p + o, chips)
        pltpu.make_async_remote_copy(
            src_ref=dw.at[m, 1 - c],
            dst_ref=from_sibling.at[m],
            send_sem=send_pair.at[m],
            recv_sem=arrive_pair.at[m],
            device_id={"dp": sibling},
            device_id_type=MESH,
        ).start()
        return carry

    def to_chip(o, carry):
        m = lax.rem(p + o, chips)
        pltpu.make_async_copy(from_sibling.at[m], from_sibling.at[m], arrive_pair.at[m]).wait()

        def add(block, inner):
            pair[m, block] = (
                dw[m, c, block].astype(F32) + from_sibling[m, block].astype(F32)
            ).astype(BF16)
            return inner

        lax.fori_loop(0, dw.shape[2], add, 0)
        pltpu.make_async_remote_copy(
            src_ref=pair.at[m],
            dst_ref=from_chips.at[o - 1],
            send_sem=send_chip.at[o - 1],
            recv_sem=arrive_chip.at[o - 1],
            device_id={"dp": 2 * m + c},
            device_id_type=MESH,
        ).start()
        return carry

    lax.fori_loop(1, chips + 1, to_sibling, 0)
    lax.fori_loop(1, chips, to_chip, 0)
    pltpu.make_async_copy(from_sibling.at[p], from_sibling.at[p], arrive_pair.at[p]).wait()


def scatter_end(p, c, dw, from_sibling, pair, from_chips, sems, out_ref):
    chips = dw.shape[0]
    send_pair, arrive_pair, send_chip, arrive_chip = sems

    def arrive(o, carry):
        pltpu.make_async_copy(from_chips.at[o], from_chips.at[o], arrive_chip.at[o]).wait()
        return carry

    def add(block, carry):
        total = dw[p, c, block].astype(F32) + from_sibling[p, block].astype(F32)
        for o in range(chips - 1):
            total = total + from_chips[o, block].astype(F32)
        out_ref[block] = total
        return carry

    def sent(o, carry):
        pltpu.make_async_copy(pair.at[o], pair.at[o], send_chip.at[o]).wait()
        return carry

    def sent_pair(m, carry):
        pltpu.make_async_copy(from_sibling.at[m], from_sibling.at[m], send_pair.at[m]).wait()
        return carry

    lax.fori_loop(0, chips - 1, arrive, 0)
    lax.fori_loop(0, dw.shape[2], add, 0)
    lax.fori_loop(0, chips - 1, sent, 0)
    lax.fori_loop(0, chips, sent_pair, 0)


def weight_terms(turned, cot, dw, channels):
    blocks = dw.shape[2]
    for tap in range(cot.shape[1] // channels):
        part = jnp.dot(
            turned,
            cot[:, tap * channels : (tap + 1) * channels],
            preferred_element_type=F32,
        ).reshape(channels // 40, 40, channels)
        for i in range(channels // 40):
            at = tap * (channels // 40) + i
            dw[at // (2 * blocks), (at // blocks) % 2, at % blocks] = part[i].astype(BF16)


def pipeline_kernel(
    sections,
    micros,
    loss_scale,
    keep_ref,
    first_ref,
    noise_ref,
    enc_gain_ref,
    dec_gain_ref,
    mix_ref,
    enc_hbm,
    dec_hbm,
    dwe_out,
    dwd_out,
    gain_out,
    enc_w,
    dec_w,
    gain_quad,
    fwd_in,
    bwd_in,
    skip_in,
    scot_in,
    dec_in,
    grad_in,
    enc_out,
    dec_out,
    grad_out,
    s_out,
    q_out,
    enc_normed,
    enc_slope,
    enc_scale,
    enc_act,
    enc_cot,
    dec_normed,
    dec_slope,
    dec_scale,
    act_out,
    h_out,
    part_out,
    act_in,
    h_in,
    part_in,
    dec_act,
    dec_cot,
    turned,
    dge_ref,
    gain_own,
    gain_pair,
    gain_sibling,
    gain_chips,
    enc_dw,
    enc_sibling,
    enc_pair,
    enc_chips,
    dec_dw,
    dec_sibling,
    dec_pair,
    dec_chips,
    local_sem,
    quad_send,
    quad_sem,
    half_send,
    half_sem,
    fwd_sem,
    bwd_sem,
    skip_sem,
    scot_sem,
    dec_sem,
    grad_sem,
    owner_send,
    owner_sem,
    enc_send,
    dec_send,
    enc_pair_sem,
    enc_chip_sem,
    dec_pair_sem,
    dec_chip_sem,
    gain_pair_sem,
    gain_chip_sem,
):
    channels = noise_ref.shape[-1]
    count = 24 * (channels // GROUPS)
    own = lax.axis_index("section")
    last = sections - 1
    quad, member = own // 4, lax.rem(own, 4)
    quads = sections // 4
    dp = lax.axis_index("dp")
    p, c = dp // 2, lax.rem(dp, 2)
    sibling = dp + 1 - 2 * c
    chips = enc_dw.shape[0]
    half_rows = dec_w.shape[1] // 2
    enc_sems = [enc_pair_sem.at[0], enc_pair_sem.at[1], enc_chip_sem.at[0], enc_chip_sem.at[1]]
    dec_sems = [dec_pair_sem.at[0], dec_pair_sem.at[1], dec_chip_sem.at[0], dec_chip_sem.at[1]]

    def remote(src, dst, send_sem, recv_sem, **device):
        return pltpu.make_async_remote_copy(
            src_ref=src,
            dst_ref=dst,
            send_sem=send_sem,
            recv_sem=recv_sem,
            device_id=device,
            device_id_type=MESH,
        )

    def wait(ref, sem):
        pltpu.make_async_copy(ref, ref, sem).wait()

    load_enc = pltpu.make_async_copy(enc_hbm, enc_w, local_sem.at[0])
    load_dec = pltpu.make_async_copy(dec_hbm, dec_w.at[member], local_sem.at[1])
    load_enc.start()
    load_dec.start()
    gain_quad[member] = jnp.broadcast_to(dec_gain_ref[...], gain_quad.shape[1:])

    barrier = pltpu.get_barrier_semaphore()

    def greet(o, carry):
        pl.semaphore_signal(
            barrier,
            inc=1,
            device_id={"section": lax.rem(own + o, sections)},
            device_id_type=MESH,
        )
        return carry

    lax.fori_loop(1, sections, greet, 0)
    pl.semaphore_signal(barrier, inc=1, device_id={"dp": sibling}, device_id_type=MESH)
    for o in range(1, chips):
        pl.semaphore_signal(
            barrier,
            inc=1,
            device_id={"dp": 2 * lax.rem(p + o, chips) + c},
            device_id_type=MESH,
        )
    pl.semaphore_wait(barrier, last + chips)

    @pl.when(own == 0)
    def _():
        for j in range(micros):
            fwd_in[j] = first_ref[j]

    half = pl.ds(pl.multiple_of(c * half_rows, half_rows), half_rows)
    other_half = pl.ds(pl.multiple_of((1 - c) * half_rows, half_rows), half_rows)

    def share(o, carry):
        to = 4 * quad + lax.rem(member + o, 4)
        remote(
            dec_hbm.at[half],
            dec_w.at[member, half],
            quad_send.at[0, o],
            quad_sem.at[0, member],
            section=to,
        ).start()
        remote(
            gain_quad.at[member],
            gain_quad.at[member],
            quad_send.at[1, o],
            quad_sem.at[1, member],
            section=to,
        ).start()
        return carry

    lax.fori_loop(1, 4, share, 0)
    dge_ref[...] = jnp.zeros_like(dge_ref)
    load_enc.wait()

    opposite = last - own
    opposite_quad, opposite_level = opposite // 4, lax.rem(opposite, 4)

    def enc_forward(j, carry):
        @pl.when(own > 0)
        def _():
            wait(fwd_in.at[j], fwd_sem.at[j])

        values = cube(fwd_in[j].astype(F32))
        keep = keep_ref[j, own].astype(F32)
        normed, scale, z, gate = norm_forward(values, enc_gain_ref[...], mix_ref, count)
        act = z * gate
        columns = spatial_taps(act, 1)
        branch = uncube(jnp.dot(columns, enc_w[...], preferred_element_type=F32))
        enc_out[j] = flat(values + keep * branch)[0]

        @pl.when(own < last)
        def _():
            remote(
                enc_out.at[j], fwd_in.at[j], enc_send.at[0, j], fwd_sem.at[j], section=own + 1
            ).start()

        pair, side = j // 2, lax.rem(j, 2)

        @pl.when(own == last)
        def _():
            remote(
                enc_out.at[j], dec_in.at[side], enc_send.at[0, j], dec_sem.at[side], section=pair
            ).start()

        remote(
            enc_out.at[j],
            skip_in.at[opposite_level, side],
            enc_send.at[1, j],
            skip_sem.at[opposite_level, side],
            section=4 * opposite_quad + pair,
        ).start()
        enc_normed[j] = normed[0]
        enc_scale[j] = scale[0]
        enc_slope[j] = (gate * (1.0 + z * (1.0 - gate)))[0]
        enc_act[pl.ds(pl.multiple_of(j * 32, 32), 32), :] = padded_rows(act)
        return carry

    lax.fori_loop(0, micros, enc_forward, 0)

    def turn_tap(tap, carry):
        rows = pl.ds(pl.multiple_of(tap * channels, channels), channels)
        enc_w[rows, :] = enc_w[rows, :].astype(F32).T.astype(BF16)
        return carry

    def pass_half(o, carry):
        of = lax.rem(member + o, 4)
        wait(dec_w.at[of, half], quad_sem.at[0, of])
        wait(gain_quad.at[of], quad_sem.at[1, of])
        remote(
            dec_w.at[of, half], dec_w.at[of, half], half_send.at[of], half_sem.at[of], dp=sibling
        ).start()
        return carry

    def take_half(o, carry):
        of = lax.rem(member + o, 4)
        wait(dec_w.at[of, other_half], half_sem.at[of])
        return carry

    load_dec.wait()
    lax.fori_loop(1, 4, pass_half, 0)
    lax.fori_loop(0, 9, turn_tap, 0)
    turned[...] = enc_act[...].astype(F32).T.astype(BF16)
    lax.fori_loop(1, 4, take_half, 0)

    mine = pl.ds(2 * member, 2)

    @pl.when(quad == 0)
    def _():
        for side in range(2):
            wait(dec_in.at[side], dec_sem.at[side])

    @pl.when(quad > 0)
    def _():
        wait(dec_in, dec_sem.at[2])

    def dec_keeps(level):
        return [
            keep_ref[2 * member + side, sections + 4 * quad + level].astype(F32)
            for side in range(2)
        ]

    def to_owner(source, target, kind, level):
        @pl.when(level != member)
        def _():
            remote(
                source.at[level],
                target,
                owner_send.at[kind, level],
                owner_sem.at[kind, member],
                section=4 * quad + level,
            ).start()

    def dec_forward(level, stream):
        for side in range(2):
            wait(skip_in.at[level, side], skip_sem.at[level, side])
        values = stream + cube(skip_in[level].astype(F32))
        normed, scale, z, gate = norm_forward(values, gain_quad[level], mix_ref, count)
        act = z * gate
        branch = uncube(
            jnp.dot(temporal_taps(act, 1), dec_w[level], preferred_element_type=F32)
        )
        result = (stream + gated(branch, dec_keeps(level))).astype(BF16).astype(F32)
        dec_normed[level] = normed
        dec_scale[level] = scale
        dec_slope[level] = gate * (1.0 + z * (1.0 - gate))
        act_out[level] = flat(act)
        to_owner(act_out, act_in.at[mine], 0, level)
        return result

    result = lax.fori_loop(0, 4, dec_forward, cube(dec_in[...].astype(F32)))

    @pl.when(quad < quads - 1)
    def _():
        dec_out[...] = flat(result)
        remote(dec_out, dec_in, dec_send.at[0], dec_sem.at[2], section=own + 4).start()
        wait(grad_in, grad_sem)

    @pl.when(quad == quads - 1)
    def _():
        gap = result - cube(noise_ref[mine].astype(F32))
        grad_in[...] = flat(gap * loss_scale)

    def dec_backward(step, upstream):
        level = 3 - step
        gate = gated(upstream, dec_keeps(level))
        h_out[level] = flat(gate)
        to_owner(h_out, h_in.at[mine], 1, level)
        columns = temporal_taps(gate, -1)
        cot = uncube(transposed_product(columns, dec_w.at[level], channels))
        grad, gain_part = norm_backward(
            cot,
            dec_normed[level],
            dec_scale[level],
            dec_slope[level],
            gain_quad[level],
            mix_ref,
            count,
        )
        s_out[level] = flat(grad)
        remote(
            s_out.at[level],
            scot_in.at[mine],
            dec_send.at[2 + level],
            scot_sem.at[member],
            section=last - 4 * quad - level,
        ).start()
        part_out[level] = gain_part
        to_owner(part_out, part_in.at[member], 2, level)
        return (upstream + grad).astype(BF16).astype(F32)

    result = lax.fori_loop(0, 4, dec_backward, cube(grad_in[...].astype(F32)))
    grad_out[...] = flat(result)

    @pl.when(quad > 0)
    def _():
        remote(grad_out, grad_in, dec_send.at[1], grad_sem, section=own - 4).start()

    @pl.when(quad == 0)
    def _():
        remote(
            grad_out, bwd_in.at[mine], dec_send.at[1], bwd_sem.at[micros + member], section=last
        ).start()

    act_in[mine] = act_out[member]
    h_in[mine] = h_out[member]
    part_in[member] = part_out[member]

    def from_member(o, carry):
        of = lax.rem(member + o, 4)
        theirs = pl.ds(2 * of, 2)
        wait(act_in.at[theirs], owner_sem.at[0, of])
        wait(h_in.at[theirs], owner_sem.at[1, of])
        wait(part_in.at[of], owner_sem.at[2, of])
        return carry

    lax.fori_loop(1, 4, from_member, 0)

    def lay_out(j, carry):
        rows = pl.ds(pl.multiple_of(j * 32, 32), 32)
        dec_act[rows, :] = padded_rows(cube(act_in[j].astype(F32)))
        dec_cot[rows, :] = temporal_taps(cube(h_in[j].astype(F32)), -1)
        return carry

    lax.fori_loop(0, micros, lay_out, 0)
    weight_terms(dec_act[...].astype(F32).T.astype(BF16), dec_cot, dec_dw, channels)
    scatter_start(p, c, sibling, dec_dw, dec_sibling, dec_pair, dec_chips, dec_sems)

    def enc_backward(j, carry):
        @pl.when(lax.rem(j, 2) == 0)
        def _():
            pair = j // 2
            both = pl.ds(j, 2)
            wait(scot_in.at[both], scot_sem.at[pair])

            @pl.when(own == last)
            def _():
                wait(bwd_in.at[both], bwd_sem.at[micros + pair])

        @pl.when(own < last)
        def _():
            wait(bwd_in.at[j], bwd_sem.at[j])

        upstream = cube(
            (bwd_in[j].astype(F32) + scot_in[j].astype(F32)).astype(BF16).astype(F32)
        )
        keep = keep_ref[j, own].astype(F32)
        columns = spatial_taps(keep * upstream, -1)
        cot = uncube(jnp.dot(columns, enc_w[...], preferred_element_type=F32))
        grad, gain_part = norm_backward(
            cot,
            enc_normed[j][None],
            enc_scale[j][None],
            enc_slope[j][None],
            enc_gain_ref[...],
            mix_ref,
            count,
        )

        @pl.when(own > 0)
        def _():
            q_out[j] = flat(upstream + grad)[0]
            remote(
                q_out.at[j], bwd_in.at[j], enc_send.at[2, j], bwd_sem.at[j], section=own - 1
            ).start()

        dge_ref[...] += gain_part
        enc_cot[pl.ds(pl.multiple_of(j * 32, 32), 32), :] = columns
        return carry

    lax.fori_loop(0, micros, enc_backward, 0)
    dgd = part_in[0] + part_in[1] + part_in[2] + part_in[3]
    row = lax.broadcasted_iota(jnp.int32, (8, channels), 0)
    gain_own[...] = jnp.where(
        row == 0,
        jnp.sum(dge_ref[...], axis=0, keepdims=True),
        jnp.where(row == 1, jnp.sum(dgd, axis=0, keepdims=True), 0.0),
    )
    to_pair = remote(
        gain_own, gain_sibling, gain_pair_sem.at[0], gain_pair_sem.at[1], dp=sibling
    )
    to_pair.start()
    weight_terms(turned[...], enc_cot, enc_dw, channels)
    scatter_start(p, c, sibling, enc_dw, enc_sibling, enc_pair, enc_chips, enc_sems)
    to_pair.wait()
    gain_pair[...] = gain_own[...] + gain_sibling[...]

    def gain_to_chip(o, carry):
        remote(
            gain_pair,
            gain_chips.at[o - 1],
            gain_chip_sem.at[0, o - 1],
            gain_chip_sem.at[1, o - 1],
            dp=2 * lax.rem(p + o, chips) + c,
        ).start()
        return carry

    lax.fori_loop(1, chips, gain_to_chip, 0)
    scatter_end(p, c, dec_dw, dec_sibling, dec_pair, dec_chips, dec_sems, dwd_out)
    scatter_end(p, c, enc_dw, enc_sibling, enc_pair, enc_chips, enc_sems, dwe_out)

    def gain_arrived(o, carry):
        for side in range(2):
            wait(gain_chips.at[o], gain_chip_sem.at[side, o])
        return carry

    lax.fori_loop(0, chips - 1, gain_arrived, 0)
    total = gain_pair[...]
    for o in range(chips - 1):
        total = total + gain_chips[o]
    gain_out[...] = total

    def drain(j, carry):
        for kind in range(2):
            wait(enc_out.at[j], enc_send.at[kind, j])

        @pl.when(own > 0)
        def _():
            wait(q_out.at[j], enc_send.at[2, j])

        return carry

    def drain_quad(o, carry):
        of = lax.rem(member + o, 4)
        wait(dec_w.at[of, half], quad_send.at[0, o])
        wait(gain_quad.at[of], quad_send.at[1, o])
        wait(dec_w.at[of, half], half_send.at[of])
        wait(act_out.at[of], owner_send.at[0, of])
        wait(h_out.at[of], owner_send.at[1, of])
        wait(part_out.at[of], owner_send.at[2, of])
        return carry

    def drain_scot(level, carry):
        wait(s_out.at[level], dec_send.at[2 + level])
        return carry

    lax.fori_loop(0, micros, drain, 0)
    lax.fori_loop(1, 4, drain_quad, 0)
    lax.fori_loop(0, 4, drain_scot, 0)
    wait(grad_out, dec_send.at[1])

    @pl.when(quad < quads - 1)
    def _():
        wait(dec_out, dec_send.at[0])


def body(
    clip_pool,
    sample_ids,
    timesteps,
    noise_draw,
    keep_lists,
    enc_weight,
    enc_gain,
    dec_weight,
    dec_gain,
):
    sections = lax.axis_size("section")
    micros = noise_draw.shape[0]
    channels = noise_draw.shape[-1]
    positions = noise_draw.shape[1] * noise_draw.shape[2] * noise_draw.shape[3]
    scale = 1.0 / math.sqrt(micros * lax.axis_size("dp") * positions)
    lined = (micros, positions, channels)
    noise = noise_draw.reshape(lined)
    clips = clip_pool.reshape((-1,) + lined[1:])
    clean = jnp.zeros(lined, F32)
    for clip in range(clips.shape[0]):
        clean = jnp.where((sample_ids == clip)[:, None, None], clips[clip][None].astype(F32), clean)
    level = noise_level(timesteps)[:, None, None]
    first = (jnp.sqrt(level) * clean + jnp.sqrt(1.0 - level) * noise.astype(F32)).astype(BF16)
    member = np.arange(channels) // (channels // GROUPS)
    mix = jnp.asarray((member[:, None] == member[None, :]).astype(np.float32), BF16)
    vmem = pl.BlockSpec(memory_space=pltpu.VMEM)
    hbm = pl.BlockSpec(memory_space=pl.ANY)
    slots = lambda *lead: pltpu.VMEM(lead + (positions, channels), BF16)
    kept = lambda *lead: pltpu.VMEM(lead + (3, 8, channels), F32)
    rows = 32 * micros
    group = lax.axis_size("dp")
    chips = group // 2
    wide = lambda *lead: pltpu.VMEM(lead + (40, channels), BF16)
    enc_blocks, dec_blocks = 9 * channels // group // 40, 3 * channels // group // 40
    shares = lambda n: [wide(chips, 2, n), wide(chips, n), wide(chips, n), wide(chips - 1, n)]
    dwe, dwd, gains = pl.pallas_call(
        lambda *refs: pipeline_kernel(sections, micros, scale, *refs),
        out_shape=(
            jax.ShapeDtypeStruct((enc_blocks, 40, channels), F32),
            jax.ShapeDtypeStruct((dec_blocks, 40, channels), F32),
            jax.ShapeDtypeStruct((8, channels), F32),
        ),
        in_specs=[pl.BlockSpec(memory_space=pltpu.SMEM), vmem, vmem, vmem, vmem, vmem, hbm, hbm],
        out_specs=(vmem, vmem, vmem),
        scratch_shapes=[
            pltpu.VMEM((9 * channels, channels), BF16),
            pltpu.VMEM((4, 3 * channels, channels), BF16),
            pltpu.VMEM((4, 8, channels), F32),
            slots(micros),
            slots(micros),
            slots(4, 2),
            slots(micros),
            slots(2),
            slots(2),
            slots(micros),
            slots(2),
            slots(2),
            slots(4, 2),
            slots(micros),
            kept(micros),
            kept(micros),
            pltpu.VMEM((micros, 8, channels), F32),
            pltpu.VMEM((rows, channels), BF16),
            pltpu.VMEM((rows, 9 * channels), BF16),
            kept(4, 2),
            kept(4, 2),
            pltpu.VMEM((4, 2, 8, channels), F32),
            slots(4, 2),
            slots(4, 2),
            pltpu.VMEM((4, 8, channels), F32),
            slots(micros),
            slots(micros),
            pltpu.VMEM((4, 8, channels), F32),
            pltpu.VMEM((rows, channels), BF16),
            pltpu.VMEM((rows, 3 * channels), BF16),
            pltpu.VMEM((channels, rows), BF16),
            pltpu.VMEM((8, channels), F32),
            pltpu.VMEM((8, channels), F32),
            pltpu.VMEM((8, channels), F32),
            pltpu.VMEM((8, channels), F32),
            pltpu.VMEM((chips - 1, 8, channels), F32),
            *shares(enc_blocks),
            *shares(dec_blocks),
            pltpu.SemaphoreType.DMA((2,)),
            pltpu.SemaphoreType.DMA((2, 4)),
            pltpu.SemaphoreType.DMA((2, 4)),
            pltpu.SemaphoreType.DMA((4,)),
            pltpu.SemaphoreType.DMA((4,)),
            pltpu.SemaphoreType.DMA((micros,)),
            pltpu.SemaphoreType.DMA((micros + 4,)),
            pltpu.SemaphoreType.DMA((4, 2)),
            pltpu.SemaphoreType.DMA((4,)),
            pltpu.SemaphoreType.DMA((3,)),
            pltpu.SemaphoreType.DMA,
            pltpu.SemaphoreType.DMA((3, 4)),
            pltpu.SemaphoreType.DMA((3, 4)),
            pltpu.SemaphoreType.DMA((3, micros)),
            pltpu.SemaphoreType.DMA((6,)),
            pltpu.SemaphoreType.DMA((2, chips)),
            pltpu.SemaphoreType.DMA((2, chips - 1)),
            pltpu.SemaphoreType.DMA((2, chips)),
            pltpu.SemaphoreType.DMA((2, chips - 1)),
            pltpu.SemaphoreType.DMA((2,)),
            pltpu.SemaphoreType.DMA((2, chips - 1)),
        ],
        compiler_params=pltpu.CompilerParams(
            collective_id=0, has_side_effects=True, vmem_limit_bytes=60 << 20
        ),
        name="pipeline",
    )(keep_lists, first, noise, enc_gain, dec_gain, mix, enc_weight[0], dec_weight[0])
    part = channels // group
    gains = lax.dynamic_slice_in_dim(gains, lax.axis_index("dp") * part, part, 1)
    return (
        dwe.reshape(1, -1, channels),
        gains[0:1],
        dwd.reshape(1, -1, channels),
        gains[1:2],
    )


def solution(mesh):
    placed = (
        P("dp", None, None, None, None),
        P("dp"),
        P("dp"),
        P("dp", None, None, None, None),
        P("dp", None),
        P("section", None, None),
        P("section", None),
        P("section", None, None),
        P("section", None),
    )
    return jax.shard_map(
        body,
        mesh=mesh,
        in_specs=placed,
        out_specs=(
            P("section", "dp", None),
            P("section", "dp"),
            P("section", "dp", None),
            P("section", "dp"),
        ),
        check_vma=False,
    )
```

```python
import math

import jax
import jax.numpy as jnp
import numpy as np
from jax import lax
from jax.experimental import pallas as pl
from jax.experimental.pallas import tpu as pltpu
from jax.sharding import PartitionSpec as P

GROUPS = 32
F32, BF16 = jnp.float32, jnp.bfloat16
MESH = pl.DeviceIdType.MESH


def noise_level(timesteps):
    phase_arg = (timesteps.astype(F32) / 1000.0 + 0.008) / 1.008
    return jnp.cos(phase_arg * (math.pi / 2.0)) ** 2


def over_rows(values):
    part = values[:, 0] + values[:, 1] + values[:, 2]
    return jnp.broadcast_to(jnp.sum(part, axis=1, keepdims=True), part.shape)


def split_terms(values):
    high = values.astype(BF16).astype(F32)
    rest = values - high
    middle = rest.astype(BF16).astype(F32)
    return [high, middle, rest - middle]


def group_means(sums, mix_ref, count):
    terms = [term for each in sums for term in split_terms(each)]
    stacked = jnp.concatenate(terms, axis=0)
    samples, rows, channels = sums[0].shape
    mixed = jnp.dot(
        stacked.reshape(-1, channels).astype(BF16), mix_ref[...], preferred_element_type=F32
    ).reshape(-1, samples, rows, channels)
    return [
        (mixed[3 * i] + mixed[3 * i + 1] + mixed[3 * i + 2]) * (1.0 / count)
        for i in range(len(sums))
    ]


def cube(values):
    return values.reshape(-1, 3, 8, values.shape[-1])


def uncube(product):
    return product.reshape(-1, 4, 8, product.shape[-1])[:, :3]


def flat(values):
    return values.reshape(-1, 24, values.shape[-1]).astype(BF16)


def padded_rows(values):
    full = jnp.concatenate([values, jnp.zeros_like(values[:, :1])], axis=1)
    return full.reshape(-1, values.shape[-1]).astype(BF16)


def spatial_taps(values, sign):
    place = lax.broadcasted_iota(jnp.int32, values.shape, 2)
    high, wide = place // 2, place % 2
    taps = []
    for tap in range(9):
        down, across = sign * (tap // 3 - 1), sign * (tap % 3 - 1)
        shift = 2 * down + across
        moved = pltpu.roll(values, (-shift) % 8, 2) if shift % 8 else values
        if down or across:
            inside = (
                (high + down >= 0) & (high + down < 4) & (wide + across >= 0) & (wide + across < 2)
            )
            moved = jnp.where(inside, moved, 0.0)
        taps.append(padded_rows(moved))
    return jnp.concatenate(taps, axis=1)


def temporal_taps(values, sign):
    zero = jnp.zeros_like(values[:, :1])
    before = jnp.concatenate([zero, values[:, :2]], axis=1)
    after = jnp.concatenate([values[:, 1:], zero], axis=1)
    taps = [before, values, after] if sign > 0 else [after, values, before]
    return jnp.concatenate([padded_rows(tap) for tap in taps], axis=1)


def norm_forward(values, gain, mix_ref, count):
    mean, square = group_means([over_rows(values), over_rows(values * values)], mix_ref, count)
    spread = jnp.maximum(square - mean * mean, 0.0)
    center = values - mean[:, None]
    scale = lax.rsqrt(spread + 1e-05)
    normed = center * scale[:, None]
    z = normed * gain[None, None]
    gate = 1.0 / (1.0 + jnp.exp(-z))
    return normed, scale, z, gate


def norm_backward(cot, normed, scale, slope, gain, mix_ref, count):
    dz = cot * slope
    gain_part = dz * normed
    gain_part = jnp.sum(gain_part[:, 0] + gain_part[:, 1] + gain_part[:, 2], axis=0)
    dn = dz * gain[None, None]
    mean_dn, mean_dnn = group_means([over_rows(dn), over_rows(dn * normed)], mix_ref, count)
    grad = scale[:, None] * (dn - mean_dn[:, None] - normed * mean_dnn[:, None])
    return grad, gain_part


def gated(values, keeps):
    return jnp.concatenate([values[s : s + 1] * keep for s, keep in enumerate(keeps)], axis=0)


def transposed_product(columns, weight_ref, channels):
    total = None
    for at in range(0, columns.shape[1], channels):
        part = lax.dot_general(
            columns[:, at : at + channels],
            weight_ref[at : at + channels, :],
            (((1,), (1,)), ((), ())),
            preferred_element_type=F32,
        )
        total = part if total is None else total + part
    return total


def scatter_start(p, c, sibling, dw, from_sibling, pair, from_chips, sems):
    chips = dw.shape[0]
    send_pair, arrive_pair, send_chip, arrive_chip = sems

    def to_sibling(o, carry):
        m = lax.rem(p + o, chips)
        pltpu.make_async_remote_copy(
            src_ref=dw.at[m, 1 - c],
            dst_ref=from_sibling.at[m],
            send_sem=send_pair.at[m],
            recv_sem=arrive_pair.at[m],
            device_id={"dp": sibling},
            device_id_type=MESH,
        ).start()
        return carry

    def to_chip(o, carry):
        m = lax.rem(p + o, chips)
        pltpu.make_async_copy(from_sibling.at[m], from_sibling.at[m], arrive_pair.at[m]).wait()

        def add(block, inner):
            pair[m, block] = (
                dw[m, c, block].astype(F32) + from_sibling[m, block].astype(F32)
            ).astype(BF16)
            return inner

        lax.fori_loop(0, dw.shape[2], add, 0)
        pltpu.make_async_remote_copy(
            src_ref=pair.at[m],
            dst_ref=from_chips.at[o - 1],
            send_sem=send_chip.at[o - 1],
            recv_sem=arrive_chip.at[o - 1],
            device_id={"dp": 2 * m + c},
            device_id_type=MESH,
        ).start()
        return carry

    lax.fori_loop(1, chips + 1, to_sibling, 0)
    lax.fori_loop(1, chips, to_chip, 0)
    pltpu.make_async_copy(from_sibling.at[p], from_sibling.at[p], arrive_pair.at[p]).wait()


def scatter_end(p, c, dw, from_sibling, pair, from_chips, sems, out_ref):
    chips = dw.shape[0]
    send_pair, arrive_pair, send_chip, arrive_chip = sems

    def arrive(o, carry):
        pltpu.make_async_copy(from_chips.at[o], from_chips.at[o], arrive_chip.at[o]).wait()
        return carry

    def add(block, carry):
        total = dw[p, c, block].astype(F32) + from_sibling[p, block].astype(F32)
        for o in range(chips - 1):
            total = total + from_chips[o, block].astype(F32)
        out_ref[block] = total
        return carry

    def sent(o, carry):
        pltpu.make_async_copy(pair.at[o], pair.at[o], send_chip.at[o]).wait()
        return carry

    def sent_pair(m, carry):
        pltpu.make_async_copy(from_sibling.at[m], from_sibling.at[m], send_pair.at[m]).wait()
        return carry

    lax.fori_loop(0, chips - 1, arrive, 0)
    lax.fori_loop(0, dw.shape[2], add, 0)
    lax.fori_loop(0, chips - 1, sent, 0)
    lax.fori_loop(0, chips, sent_pair, 0)


def weight_terms(turned, cot, dw, channels):
    blocks = dw.shape[2]
    for tap in range(cot.shape[1] // channels):
        part = jnp.dot(
            turned,
            cot[:, tap * channels : (tap + 1) * channels],
            preferred_element_type=F32,
        ).reshape(channels // 40, 40, channels)
        for i in range(channels // 40):
            at = tap * (channels // 40) + i
            dw[at // (2 * blocks), (at // blocks) % 2, at % blocks] = part[i].astype(BF16)


def pipeline_kernel(
    sections,
    micros,
    loss_scale,
    keep_ref,
    first_ref,
    noise_ref,
    enc_gain_ref,
    dec_gain_ref,
    mix_ref,
    enc_hbm,
    dec_hbm,
    dwe_out,
    dwd_out,
    gain_out,
    enc_w,
    dec_w,
    keep_used,
    noise_used,
    gain_quad,
    fwd_in,
    bwd_in,
    skip_in,
    scot_in,
    dec_in,
    grad_in,
    enc_out,
    dec_out,
    grad_out,
    s_out,
    q_out,
    enc_normed,
    enc_slope,
    enc_scale,
    enc_act,
    enc_cot,
    dec_normed,
    dec_slope,
    dec_scale,
    act_out,
    h_out,
    part_out,
    act_in,
    h_in,
    part_in,
    dec_act,
    dec_cot,
    product,
    turned,
    dge_ref,
    gain_own,
    gain_pair,
    gain_sibling,
    gain_chips,
    enc_dw,
    enc_sibling,
    enc_pair,
    enc_chips,
    dec_dw,
    dec_sibling,
    dec_pair,
    dec_chips,
    local_sem,
    quad_send,
    quad_sem,
    half_send,
    half_sem,
    fwd_sem,
    bwd_sem,
    skip_sem,
    scot_sem,
    dec_sem,
    grad_sem,
    owner_send,
    owner_sem,
    enc_send,
    dec_send,
    enc_pair_sem,
    enc_chip_sem,
    dec_pair_sem,
    dec_chip_sem,
    gain_pair_sem,
    gain_chip_sem,
):
    channels = noise_ref.shape[-1]
    count = 24 * (channels // GROUPS)
    own = lax.axis_index("section")
    last = sections - 1
    quad, member = own // 4, lax.rem(own, 4)
    quads = sections // 4
    dp = lax.axis_index("dp")
    p, c = dp // 2, lax.rem(dp, 2)
    sibling = dp + 1 - 2 * c
    across = 2 - 4 * lax.rem(p, 2)
    odd = lax.rem(own, 2)
    chips = enc_dw.shape[0]
    half_rows = dec_w.shape[1] // 2
    enc_sems = [enc_pair_sem.at[0], enc_pair_sem.at[1], enc_chip_sem.at[0], enc_chip_sem.at[1]]
    dec_sems = [dec_pair_sem.at[0], dec_pair_sem.at[1], dec_chip_sem.at[0], dec_chip_sem.at[1]]

    def remote(src, dst, send_sem, recv_sem, **device):
        return pltpu.make_async_remote_copy(
            src_ref=src,
            dst_ref=dst,
            send_sem=send_sem,
            recv_sem=recv_sem,
            device_id=device,
            device_id_type=MESH,
        )

    def at(section):
        return {"section": section, "dp": dp + across * lax.rem(section + own, 2)}

    def wait(ref, sem):
        pltpu.make_async_copy(ref, ref, sem).wait()

    load_enc = pltpu.make_async_copy(enc_hbm, enc_w, local_sem.at[0])
    load_dec = pltpu.make_async_copy(dec_hbm, dec_w.at[member], local_sem.at[1])
    load_enc.start()
    load_dec.start()
    gain_quad[member] = jnp.broadcast_to(dec_gain_ref[...], gain_quad.shape[1:])

    barrier = pltpu.get_barrier_semaphore()

    def greet(o, carry):
        pl.semaphore_signal(
            barrier,
            inc=1,
            device_id=at(lax.rem(own + o, sections)),
            device_id_type=MESH,
        )
        return carry

    lax.fori_loop(1, sections, greet, 0)
    pl.semaphore_signal(barrier, inc=1, device_id={"dp": sibling}, device_id_type=MESH)
    for o in range(1, chips):
        pl.semaphore_signal(
            barrier,
            inc=1,
            device_id={"dp": 2 * lax.rem(p + o, chips) + c},
            device_id_type=MESH,
        )
    pl.semaphore_wait(barrier, last + chips)

    @pl.when(own == 0)
    def _():
        for j in range(micros):
            fwd_in[j] = first_ref[j]

    @pl.when(odd == 1)
    def _():
        remote(keep_ref, keep_used, local_sem.at[2], local_sem.at[3], dp=dp + across).start()

        @pl.when(quad == quads - 1)
        def _():
            remote(noise_ref, noise_used, local_sem.at[4], local_sem.at[5], dp=dp + across).start()

        wait(keep_used, local_sem.at[3])

    @pl.when(odd == 0)
    def _():
        keep_used[...] = keep_ref[...]

        @pl.when(quad == quads - 1)
        def _():
            noise_used[...] = noise_ref[...]

    def kept_at(sample, level):
        row = keep_used[sample, pl.ds(level, 1), :]
        return jnp.concatenate([row] * (channels // row.shape[-1]), axis=1)

    half = pl.ds(pl.multiple_of(c * half_rows, half_rows), half_rows)
    other_half = pl.ds(pl.multiple_of((1 - c) * half_rows, half_rows), half_rows)

    def share(o, carry):
        to = 4 * quad + lax.rem(member + o, 4)
        remote(
            dec_hbm.at[half],
            dec_w.at[member, half],
            quad_send.at[0, o],
            quad_sem.at[0, member],
            **at(to),
        ).start()
        remote(
            gain_quad.at[member],
            gain_quad.at[member],
            quad_send.at[1, o],
            quad_sem.at[1, member],
            **at(to),
        ).start()
        return carry

    @pl.when(own >= sections // 2)
    def _():
        lax.fori_loop(1, 4, share, 0)

    dge_ref[...] = jnp.zeros_like(dge_ref)
    load_enc.wait()

    opposite = last - own
    opposite_quad, opposite_level = opposite // 4, lax.rem(opposite, 4)

    def enc_forward(j, carry):
        @pl.when(own > 0)
        def _():
            wait(fwd_in.at[j], fwd_sem.at[j])

        values = cube(fwd_in[j].astype(F32))
        keep = kept_at(j, own)
        normed, scale, z, gate = norm_forward(values, enc_gain_ref[...], mix_ref, count)
        act = z * gate
        columns = spatial_taps(act, 1)
        branch = uncube(jnp.dot(columns, enc_w[...], preferred_element_type=F32))
        enc_out[j] = flat(values + keep * branch)[0]

        @pl.when(own < last)
        def _():
            remote(
                enc_out.at[j], fwd_in.at[j], enc_send.at[0, j], fwd_sem.at[j], **at(own + 1)
            ).start()

        pair, side = j // 2, lax.rem(j, 2)

        @pl.when(own == last)
        def _():
            remote(
                enc_out.at[j], dec_in.at[side], enc_send.at[0, j], dec_sem.at[side], **at(pair)
            ).start()

        remote(
            enc_out.at[j],
            skip_in.at[opposite_level, side],
            enc_send.at[1, j],
            skip_sem.at[opposite_level, side],
            **at(4 * opposite_quad + pair),
        ).start()
        enc_normed[j] = normed[0]
        enc_scale[j] = scale[0]
        enc_slope[j] = (gate * (1.0 + z * (1.0 - gate)))[0]
        enc_act[pl.ds(pl.multiple_of(j * 32, 32), 32), :] = padded_rows(act)
        return carry

    lax.fori_loop(0, micros, enc_forward, 0)

    @pl.when(own < sections // 2)
    def _():
        lax.fori_loop(1, 4, share, 0)

    def turn_tap(tap, carry):
        rows = pl.ds(pl.multiple_of(tap * channels, channels), channels)
        enc_w[rows, :] = enc_w[rows, :].astype(F32).T.astype(BF16)
        return carry

    def pass_half(o, carry):
        of = lax.rem(member + o, 4)
        wait(dec_w.at[of, half], quad_sem.at[0, of])
        wait(gain_quad.at[of], quad_sem.at[1, of])
        remote(
            dec_w.at[of, half], dec_w.at[of, half], half_send.at[of], half_sem.at[of], dp=sibling
        ).start()
        return carry

    def take_half(o, carry):
        of = lax.rem(member + o, 4)
        wait(dec_w.at[of, other_half], half_sem.at[of])
        return carry

    load_dec.wait()
    lax.fori_loop(1, 4, pass_half, 0)
    lax.fori_loop(0, 9, turn_tap, 0)
    turned[...] = enc_act[...].astype(F32).T.astype(BF16)
    lax.fori_loop(1, 4, take_half, 0)

    mine = pl.ds(2 * member, 2)

    @pl.when(quad == 0)
    def _():
        for side in range(2):
            wait(dec_in.at[side], dec_sem.at[side])

    @pl.when(quad > 0)
    def _():
        wait(dec_in, dec_sem.at[2])

    def dec_keeps(level):
        return [
            kept_at(2 * member + side, sections + 4 * quad + level)
            for side in range(2)
        ]

    def to_owner(source, target, kind, level):
        @pl.when(level != member)
        def _():
            remote(
                source.at[level],
                target,
                owner_send.at[kind, level],
                owner_sem.at[kind, member],
                **at(4 * quad + level),
            ).start()

    def dec_forward(level, stream):
        for side in range(2):
            wait(skip_in.at[level, side], skip_sem.at[level, side])
        values = stream + cube(skip_in[level].astype(F32))
        normed, scale, z, gate = norm_forward(values, gain_quad[level], mix_ref, count)
        act = z * gate
        branch = uncube(
            jnp.dot(temporal_taps(act, 1), dec_w[level], preferred_element_type=F32)
        )
        result = (stream + gated(branch, dec_keeps(level))).astype(BF16).astype(F32)
        dec_normed[level] = normed
        dec_scale[level] = scale
        dec_slope[level] = gate * (1.0 + z * (1.0 - gate))
        act_out[level] = flat(act)
        to_owner(act_out, act_in.at[mine], 0, level)
        return result

    result = lax.fori_loop(0, 4, dec_forward, cube(dec_in[...].astype(F32)))

    def halves_left(o, carry):
        of = lax.rem(member + o, 4)
        wait(dec_w.at[of, half], half_send.at[of])
        return carry

    lax.fori_loop(1, 4, halves_left, 0)

    def turn_dec(tap, carry):
        level = tap // 3
        rows = pl.ds(pl.multiple_of(lax.rem(tap, 3) * channels, channels), channels)
        dec_w[level, rows, :] = dec_w[level, rows, :].astype(F32).T.astype(BF16)
        return carry

    @pl.when(quad < quads - 1)
    def _():
        dec_out[...] = flat(result)
        remote(dec_out, dec_in, dec_send.at[0], dec_sem.at[2], **at(own + 4)).start()
        lax.fori_loop(0, 12, turn_dec, 0)
        wait(grad_in, grad_sem)

    @pl.when(quad == quads - 1)
    def _():
        @pl.when(odd == 1)
        def _():
            wait(noise_used, local_sem.at[5])

        gap = result - cube(noise_used[mine].astype(F32))
        grad_in[...] = flat(gap * loss_scale)

    def dec_backward(step, upstream):
        level = 3 - step
        gate = gated(upstream, dec_keeps(level))
        h_out[level] = flat(gate)
        to_owner(h_out, h_in.at[mine], 1, level)
        columns = temporal_taps(gate, -1)

        @pl.when(quad < quads - 1)
        def _():
            product[...] = jnp.dot(columns, dec_w[level], preferred_element_type=F32)

        @pl.when(quad == quads - 1)
        def _():
            product[...] = transposed_product(columns, dec_w.at[level], channels)

        cot = uncube(product[...])
        grad, gain_part = norm_backward(
            cot,
            dec_normed[level],
            dec_scale[level],
            dec_slope[level],
            gain_quad[level],
            mix_ref,
            count,
        )
        s_out[level] = flat(grad)
        remote(
            s_out.at[level],
            scot_in.at[mine],
            dec_send.at[2 + level],
            scot_sem.at[member],
            **at(last - 4 * quad - level),
        ).start()
        part_out[level] = gain_part
        to_owner(part_out, part_in.at[member], 2, level)
        return (upstream + grad).astype(BF16).astype(F32)

    result = lax.fori_loop(0, 4, dec_backward, cube(grad_in[...].astype(F32)))
    grad_out[...] = flat(result)

    @pl.when(quad > 0)
    def _():
        remote(grad_out, grad_in, dec_send.at[1], grad_sem, **at(own - 4)).start()

    @pl.when(quad == 0)
    def _():
        remote(
            grad_out, bwd_in.at[mine], dec_send.at[1], bwd_sem.at[micros + member], **at(last)
        ).start()

    act_in[mine] = act_out[member]
    h_in[mine] = h_out[member]
    part_in[member] = part_out[member]

    def from_member(o, carry):
        of = lax.rem(member + o, 4)
        theirs = pl.ds(2 * of, 2)
        wait(act_in.at[theirs], owner_sem.at[0, of])
        wait(h_in.at[theirs], owner_sem.at[1, of])
        wait(part_in.at[of], owner_sem.at[2, of])
        return carry

    lax.fori_loop(1, 4, from_member, 0)

    def lay_out(j, carry):
        rows = pl.ds(pl.multiple_of(j * 32, 32), 32)
        dec_act[rows, :] = padded_rows(cube(act_in[j].astype(F32)))
        dec_cot[rows, :] = temporal_taps(cube(h_in[j].astype(F32)), -1)
        return carry

    lax.fori_loop(0, micros, lay_out, 0)
    weight_terms(dec_act[...].astype(F32).T.astype(BF16), dec_cot, dec_dw, channels)
    scatter_start(p, c, sibling, dec_dw, dec_sibling, dec_pair, dec_chips, dec_sems)

    def enc_backward(j, carry):
        @pl.when(lax.rem(j, 2) == 0)
        def _():
            pair = j // 2
            both = pl.ds(j, 2)
            wait(scot_in.at[both], scot_sem.at[pair])

            @pl.when(own == last)
            def _():
                wait(bwd_in.at[both], bwd_sem.at[micros + pair])

        @pl.when(own < last)
        def _():
            wait(bwd_in.at[j], bwd_sem.at[j])

        upstream = cube(
            (bwd_in[j].astype(F32) + scot_in[j].astype(F32)).astype(BF16).astype(F32)
        )
        keep = kept_at(j, own)
        columns = spatial_taps(keep * upstream, -1)
        cot = uncube(jnp.dot(columns, enc_w[...], preferred_element_type=F32))
        grad, gain_part = norm_backward(
            cot,
            enc_normed[j][None],
            enc_scale[j][None],
            enc_slope[j][None],
            enc_gain_ref[...],
            mix_ref,
            count,
        )

        @pl.when(own > 0)
        def _():
            q_out[j] = flat(upstream + grad)[0]
            remote(
                q_out.at[j], bwd_in.at[j], enc_send.at[2, j], bwd_sem.at[j], **at(own - 1)
            ).start()

        dge_ref[...] += gain_part
        enc_cot[pl.ds(pl.multiple_of(j * 32, 32), 32), :] = columns
        return carry

    lax.fori_loop(0, micros, enc_backward, 0)
    dgd = part_in[0] + part_in[1] + part_in[2] + part_in[3]
    row = lax.broadcasted_iota(jnp.int32, (8, channels), 0)
    gain_own[...] = jnp.where(
        row == 0,
        jnp.sum(dge_ref[...], axis=0, keepdims=True),
        jnp.where(row == 1, jnp.sum(dgd, axis=0, keepdims=True), 0.0),
    )
    to_pair = remote(
        gain_own, gain_sibling, gain_pair_sem.at[0], gain_pair_sem.at[1], dp=sibling
    )
    to_pair.start()
    weight_terms(turned[...], enc_cot, enc_dw, channels)
    scatter_start(p, c, sibling, enc_dw, enc_sibling, enc_pair, enc_chips, enc_sems)
    to_pair.wait()
    gain_pair[...] = gain_own[...] + gain_sibling[...]

    def gain_to_chip(o, carry):
        remote(
            gain_pair,
            gain_chips.at[o - 1],
            gain_chip_sem.at[0, o - 1],
            gain_chip_sem.at[1, o - 1],
            dp=2 * lax.rem(p + o, chips) + c,
        ).start()
        return carry

    lax.fori_loop(1, chips, gain_to_chip, 0)
    scatter_end(p, c, dec_dw, dec_sibling, dec_pair, dec_chips, dec_sems, dwd_out)
    scatter_end(p, c, enc_dw, enc_sibling, enc_pair, enc_chips, enc_sems, dwe_out)

    def gain_arrived(o, carry):
        for side in range(2):
            wait(gain_chips.at[o], gain_chip_sem.at[side, o])
        return carry

    lax.fori_loop(0, chips - 1, gain_arrived, 0)
    total = gain_pair[...]
    for o in range(chips - 1):
        total = total + gain_chips[o]
    gain_out[...] = total

    def drain(j, carry):
        for kind in range(2):
            wait(enc_out.at[j], enc_send.at[kind, j])

        @pl.when(own > 0)
        def _():
            wait(q_out.at[j], enc_send.at[2, j])

        return carry

    def drain_quad(o, carry):
        of = lax.rem(member + o, 4)
        wait(dec_w.at[of, half], quad_send.at[0, o])
        wait(gain_quad.at[of], quad_send.at[1, o])
        wait(act_out.at[of], owner_send.at[0, of])
        wait(h_out.at[of], owner_send.at[1, of])
        wait(part_out.at[of], owner_send.at[2, of])
        return carry

    def drain_scot(level, carry):
        wait(s_out.at[level], dec_send.at[2 + level])
        return carry

    lax.fori_loop(0, micros, drain, 0)
    lax.fori_loop(1, 4, drain_quad, 0)
    lax.fori_loop(0, 4, drain_scot, 0)
    wait(grad_out, dec_send.at[1])

    @pl.when(quad < quads - 1)
    def _():
        wait(dec_out, dec_send.at[0])

    @pl.when(odd == 1)
    def _():
        wait(keep_used, local_sem.at[2])

        @pl.when(quad == quads - 1)
        def _():
            wait(noise_used, local_sem.at[4])


def body(
    clip_pool,
    sample_ids,
    timesteps,
    noise_draw,
    keep_lists,
    enc_weight,
    enc_gain,
    dec_weight,
    dec_gain,
):
    sections = lax.axis_size("section")
    micros = noise_draw.shape[0]
    channels = noise_draw.shape[-1]
    positions = noise_draw.shape[1] * noise_draw.shape[2] * noise_draw.shape[3]
    scale = 1.0 / math.sqrt(micros * lax.axis_size("dp") * positions)
    lined = (micros, positions, channels)
    noise = noise_draw.reshape(lined)
    clips = clip_pool.reshape((-1,) + lined[1:])
    clean = jnp.zeros(lined, F32)
    for clip in range(clips.shape[0]):
        clean = jnp.where((sample_ids == clip)[:, None, None], clips[clip][None].astype(F32), clean)
    level = noise_level(timesteps)[:, None, None]
    first = (jnp.sqrt(level) * clean + jnp.sqrt(1.0 - level) * noise.astype(F32)).astype(BF16)
    keeps = jnp.broadcast_to(keep_lists.astype(F32)[:, :, None], keep_lists.shape + (128,))
    member = np.arange(channels) // (channels // GROUPS)
    mix = jnp.asarray((member[:, None] == member[None, :]).astype(np.float32), BF16)
    vmem = pl.BlockSpec(memory_space=pltpu.VMEM)
    hbm = pl.BlockSpec(memory_space=pl.ANY)
    slots = lambda *lead: pltpu.VMEM(lead + (positions, channels), BF16)
    kept = lambda *lead: pltpu.VMEM(lead + (3, 8, channels), F32)
    rows = 32 * micros
    group = lax.axis_size("dp")
    chips = group // 2
    wide = lambda *lead: pltpu.VMEM(lead + (40, channels), BF16)
    enc_blocks, dec_blocks = 9 * channels // group // 40, 3 * channels // group // 40
    shares = lambda n: [wide(chips, 2, n), wide(chips, n), wide(chips, n), wide(chips - 1, n)]
    dwe, dwd, gains = pl.pallas_call(
        lambda *refs: pipeline_kernel(sections, micros, scale, *refs),
        out_shape=(
            jax.ShapeDtypeStruct((enc_blocks, 40, channels), F32),
            jax.ShapeDtypeStruct((dec_blocks, 40, channels), F32),
            jax.ShapeDtypeStruct((8, channels), F32),
        ),
        in_specs=[vmem, vmem, vmem, vmem, vmem, vmem, hbm, hbm],
        out_specs=(vmem, vmem, vmem),
        scratch_shapes=[
            pltpu.VMEM((9 * channels, channels), BF16),
            pltpu.VMEM((4, 3 * channels, channels), BF16),
            pltpu.VMEM((micros, 2 * sections, 128), F32),
            slots(micros),
            pltpu.VMEM((4, 8, channels), F32),
            slots(micros),
            slots(micros),
            slots(4, 2),
            slots(micros),
            slots(2),
            slots(2),
            slots(micros),
            slots(2),
            slots(2),
            slots(4, 2),
            slots(micros),
            kept(micros),
            kept(micros),
            pltpu.VMEM((micros, 8, channels), F32),
            pltpu.VMEM((rows, channels), BF16),
            pltpu.VMEM((rows, 9 * channels), BF16),
            kept(4, 2),
            kept(4, 2),
            pltpu.VMEM((4, 2, 8, channels), F32),
            slots(4, 2),
            slots(4, 2),
            pltpu.VMEM((4, 8, channels), F32),
            slots(micros),
            slots(micros),
            pltpu.VMEM((4, 8, channels), F32),
            pltpu.VMEM((rows, channels), BF16),
            pltpu.VMEM((rows, 3 * channels), BF16),
            pltpu.VMEM((64, channels), F32),
            pltpu.VMEM((channels, rows), BF16),
            pltpu.VMEM((8, channels), F32),
            pltpu.VMEM((8, channels), F32),
            pltpu.VMEM((8, channels), F32),
            pltpu.VMEM((8, channels), F32),
            pltpu.VMEM((chips - 1, 8, channels), F32),
            *shares(enc_blocks),
            *shares(dec_blocks),
            pltpu.SemaphoreType.DMA((6,)),
            pltpu.SemaphoreType.DMA((2, 4)),
            pltpu.SemaphoreType.DMA((2, 4)),
            pltpu.SemaphoreType.DMA((4,)),
            pltpu.SemaphoreType.DMA((4,)),
            pltpu.SemaphoreType.DMA((micros,)),
            pltpu.SemaphoreType.DMA((micros + 4,)),
            pltpu.SemaphoreType.DMA((4, 2)),
            pltpu.SemaphoreType.DMA((4,)),
            pltpu.SemaphoreType.DMA((3,)),
            pltpu.SemaphoreType.DMA,
            pltpu.SemaphoreType.DMA((3, 4)),
            pltpu.SemaphoreType.DMA((3, 4)),
            pltpu.SemaphoreType.DMA((3, micros)),
            pltpu.SemaphoreType.DMA((6,)),
            pltpu.SemaphoreType.DMA((2, chips)),
            pltpu.SemaphoreType.DMA((2, chips - 1)),
            pltpu.SemaphoreType.DMA((2, chips)),
            pltpu.SemaphoreType.DMA((2, chips - 1)),
            pltpu.SemaphoreType.DMA((2,)),
            pltpu.SemaphoreType.DMA((2, chips - 1)),
        ],
        compiler_params=pltpu.CompilerParams(
            collective_id=0, has_side_effects=True, vmem_limit_bytes=60 << 20
        ),
        name="pipeline",
    )(keeps, first, noise, enc_gain, dec_gain, mix, enc_weight[0], dec_weight[0])
    part = channels // group
    gains = lax.dynamic_slice_in_dim(gains, lax.axis_index("dp") * part, part, 1)
    return (
        dwe.reshape(1, -1, channels),
        gains[0:1],
        dwd.reshape(1, -1, channels),
        gains[1:2],
    )


def solution(mesh):
    placed = (
        P("dp", None, None, None, None),
        P("dp"),
        P("dp"),
        P("dp", None, None, None, None),
        P("dp", None),
        P("section", None, None),
        P("section", None),
        P("section", None, None),
        P("section", None),
    )
    return jax.shard_map(
        body,
        mesh=mesh,
        in_specs=placed,
        out_specs=(
            P("section", "dp", None),
            P("section", "dp"),
            P("section", "dp", None),
            P("section", "dp"),
        ),
        check_vma=False,
    )
```

```python
import math

import jax
import jax.numpy as jnp
import numpy as np
from jax import lax
from jax.experimental import pallas as pl
from jax.experimental.pallas import tpu as pltpu
from jax.sharding import PartitionSpec as P

GROUPS = 32
F32, BF16 = jnp.float32, jnp.bfloat16
MESH = pl.DeviceIdType.MESH


def noise_level(timesteps):
    phase_arg = (timesteps.astype(F32) / 1000.0 + 0.008) / 1.008
    return jnp.cos(phase_arg * (math.pi / 2.0)) ** 2


def over_rows(values):
    part = values[:, 0] + values[:, 1] + values[:, 2]
    return jnp.broadcast_to(jnp.sum(part, axis=1, keepdims=True), part.shape)


def split_terms(values):
    high = values.astype(BF16).astype(F32)
    rest = values - high
    middle = rest.astype(BF16).astype(F32)
    return [high, middle, rest - middle]


def group_means(sums, mix_ref, count):
    terms = [term for each in sums for term in split_terms(each)]
    stacked = jnp.concatenate(terms, axis=0)
    samples, rows, channels = sums[0].shape
    mixed = jnp.dot(
        stacked.reshape(-1, channels).astype(BF16), mix_ref[...], preferred_element_type=F32
    ).reshape(-1, samples, rows, channels)
    return [
        (mixed[3 * i] + mixed[3 * i + 1] + mixed[3 * i + 2]) * (1.0 / count)
        for i in range(len(sums))
    ]


def cube(values):
    return values.reshape(-1, 3, 8, values.shape[-1])


def uncube(product):
    return product.reshape(-1, 4, 8, product.shape[-1])[:, :3]


def flat(values):
    return values.reshape(-1, 24, values.shape[-1]).astype(BF16)


def padded_rows(values):
    full = jnp.concatenate([values, jnp.zeros_like(values[:, :1])], axis=1)
    return full.reshape(-1, values.shape[-1]).astype(BF16)


def spatial_taps(values, sign):
    place = lax.broadcasted_iota(jnp.int32, values.shape, 2)
    high, wide = place // 2, place % 2
    taps = []
    for tap in range(9):
        down, across = sign * (tap // 3 - 1), sign * (tap % 3 - 1)
        shift = 2 * down + across
        moved = pltpu.roll(values, (-shift) % 8, 2) if shift % 8 else values
        if down or across:
            inside = (
                (high + down >= 0) & (high + down < 4) & (wide + across >= 0) & (wide + across < 2)
            )
            moved = jnp.where(inside, moved, 0.0)
        taps.append(padded_rows(moved))
    return jnp.concatenate(taps, axis=1)


def temporal_taps(values, sign):
    zero = jnp.zeros_like(values[:, :1])
    before = jnp.concatenate([zero, values[:, :2]], axis=1)
    after = jnp.concatenate([values[:, 1:], zero], axis=1)
    taps = [before, values, after] if sign > 0 else [after, values, before]
    return jnp.concatenate([padded_rows(tap) for tap in taps], axis=1)


def norm_forward(values, gain, mix_ref, count):
    mean, square = group_means([over_rows(values), over_rows(values * values)], mix_ref, count)
    spread = jnp.maximum(square - mean * mean, 0.0)
    center = values - mean[:, None]
    scale = lax.rsqrt(spread + 1e-05)
    normed = center * scale[:, None]
    z = normed * gain[None, None]
    gate = 1.0 / (1.0 + jnp.exp(-z))
    return normed, scale, z, gate


def norm_backward(cot, normed, scale, slope, gain, mix_ref, count):
    dz = cot * slope
    gain_part = dz * normed
    gain_part = jnp.sum(gain_part[:, 0] + gain_part[:, 1] + gain_part[:, 2], axis=0)
    dn = dz * gain[None, None]
    mean_dn, mean_dnn = group_means([over_rows(dn), over_rows(dn * normed)], mix_ref, count)
    grad = scale[:, None] * (dn - mean_dn[:, None] - normed * mean_dnn[:, None])
    return grad, gain_part


def gated(values, keeps):
    return jnp.concatenate([values[s : s + 1] * keep for s, keep in enumerate(keeps)], axis=0)


def transposed_product(columns, weight_ref, channels):
    total = None
    for at in range(0, columns.shape[1], channels):
        part = lax.dot_general(
            columns[:, at : at + channels],
            weight_ref[at : at + channels, :],
            (((1,), (1,)), ((), ())),
            preferred_element_type=F32,
        )
        total = part if total is None else total + part
    return total


def halving(p):
    y, x = p // 2, lax.rem(p, 2)
    ring = lambda row: lax.rem((row + 1) // 2, 2)
    side, half = ring(y), y // 2
    next_y = y + 1 - 2 * lax.rem(y, 2)
    far_y = 3 - y
    row = lambda which, i: which + i * (3 - 2 * which)
    over_x, over_a, over_b = 2 * y + 1 - x, 2 * next_y + x, 2 * far_y + x
    return [
        dict(
            partners=[over_x, over_a, over_b],
            kept=[lambda i: 2 * i + x, lambda i: 2 * row(side, i) + x],
            sent=lambda i: 2 * row(1 - side, i) + x,
            goes=lambda m: (lax.rem(m, 2) != x, m // 2),
        ),
        dict(
            partners=[over_a, over_b, over_x],
            kept=[lambda i: 2 * row(side, i // 2) + lax.rem(i, 2), lambda i: 2 * y + i],
            sent=lambda i: 2 * far_y + i,
            goes=lambda m: (ring(m // 2) != side, 2 * (m // 4) + lax.rem(m, 2)),
        ),
        dict(
            partners=[over_b, over_x, over_a],
            kept=[lambda i: 4 * half + i, lambda i: 2 * (2 * half + i) + x],
            sent=lambda i: 2 * (2 * half + i) + 1 - x,
            goes=lambda m: (m // 4 != half, lax.rem(m, 4)),
        ),
    ]


def chip_copy(c, third, src, place, buffers, sems, partner):
    _, _, pair, from_chips = buffers
    width = pair.shape[1] // 3
    blocks = pl.ds(third * width, width)
    return pltpu.make_async_remote_copy(
        src_ref=pair.at[src, blocks],
        dst_ref=from_chips.at[place, blocks],
        send_sem=sems[2].at[third, place],
        recv_sem=sems[3].at[third, place],
        device_id={"dp": 2 * partner + c},
        device_id_type=MESH,
    )


def wait_third(from_chips, third, place, sem):
    width = from_chips.shape[1] // 3
    ref = from_chips.at[place, pl.ds(third * width, width)]
    pltpu.make_async_copy(ref, ref, sem.at[third, place]).wait()


def scatter_start(p, c, sibling, buffers, sems):
    dw, from_sibling, pair, from_chips = buffers
    chips = dw.shape[0]
    send_pair, arrive_pair, _, _ = sems
    orders = halving(p)

    def to_sibling(o, carry):
        m = lax.rem(p + o, chips)
        pltpu.make_async_remote_copy(
            src_ref=dw.at[m, 1 - c],
            dst_ref=from_sibling.at[m],
            send_sem=send_pair.at[m],
            recv_sem=arrive_pair.at[m],
            device_id={"dp": sibling},
            device_id_type=MESH,
        ).start()
        return carry

    def add_pair(o, carry):
        m = lax.rem(p + o, chips)
        pltpu.make_async_copy(from_sibling.at[m], from_sibling.at[m], arrive_pair.at[m]).wait()

        def add(block, inner):
            pair[m, block] = (
                dw[m, c, block].astype(F32) + from_sibling[m, block].astype(F32)
            ).astype(BF16)
            return inner

        lax.fori_loop(0, dw.shape[2], add, 0)
        for third, order in enumerate(orders):
            goes, place = order["goes"](m)

            @pl.when(goes)
            def _():
                chip_copy(c, third, m, place, buffers, sems, order["partners"][0]).start()

        return carry

    lax.fori_loop(1, chips + 1, to_sibling, 0)
    lax.fori_loop(1, chips + 1, add_pair, 0)


def scatter_step(p, c, buffers, sems, step):
    _, _, pair, from_chips = buffers
    width = pair.shape[1] // 3
    base = 4 * step
    for third, order in enumerate(halving(p)):

        def take(i, carry):
            wait_third(from_chips, third, base + i, sems[3])
            kept = order["kept"][step](i)

            def add(n, inner):
                block = third * width + n
                pair[kept, block] = (
                    pair[kept, block].astype(F32) + from_chips[base + i, block].astype(F32)
                ).astype(BF16)
                return inner

            lax.fori_loop(0, width, add, 0)
            return carry

        lax.fori_loop(0, 4 if step == 0 else 2, take, 0)
        if step == 0:
            for i in range(2):
                chip_copy(
                    c, third, order["sent"](i), 4 + i, buffers, sems, order["partners"][1]
                ).start()
        else:
            partner = order["partners"][2]
            chip_copy(c, third, partner, 6, buffers, sems, partner).start()


def scatter_end(p, c, buffers, sems, out_ref):
    _, from_sibling, pair, from_chips = buffers
    chips = pair.shape[0]
    width = pair.shape[1] // 3
    for third in range(3):
        wait_third(from_chips, third, 6, sems[3])

        def add(n, carry):
            block = third * width + n
            out_ref[block] = pair[p, block].astype(F32) + from_chips[6, block].astype(F32)
            return carry

        lax.fori_loop(0, width, add, 0)

    def sent(place, carry):
        for third in range(3):
            wait_third(from_chips, third, place, sems[2])
        return carry

    def sent_pair(m, carry):
        pltpu.make_async_copy(from_sibling.at[m], from_sibling.at[m], sems[0].at[m]).wait()
        return carry

    lax.fori_loop(0, chips - 1, sent, 0)
    lax.fori_loop(0, chips, sent_pair, 0)


def weight_terms(turned, cot, dw, channels):
    blocks = dw.shape[2]
    for tap in range(cot.shape[1] // channels):
        part = jnp.dot(
            turned,
            cot[:, tap * channels : (tap + 1) * channels],
            preferred_element_type=F32,
        ).reshape(channels // 40, 40, channels)
        for i in range(channels // 40):
            at = tap * (channels // 40) + i
            dw[at // (2 * blocks), (at // blocks) % 2, at % blocks] = part[i].astype(BF16)


def pipeline_kernel(
    sections,
    micros,
    loss_scale,
    keep_ref,
    first_ref,
    noise_ref,
    enc_gain_ref,
    dec_gain_ref,
    mix_ref,
    enc_hbm,
    dec_hbm,
    dwe_out,
    dwd_out,
    gain_out,
    enc_w,
    dec_w,
    keep_used,
    noise_used,
    gain_quad,
    fwd_in,
    bwd_in,
    skip_in,
    scot_in,
    dec_in,
    grad_in,
    enc_out,
    dec_out,
    grad_out,
    s_out,
    q_out,
    enc_normed,
    enc_slope,
    enc_scale,
    enc_act,
    enc_cot,
    dec_normed,
    dec_slope,
    dec_scale,
    act_out,
    h_out,
    part_out,
    act_in,
    h_in,
    part_in,
    dec_act,
    dec_cot,
    product,
    turned,
    dge_ref,
    gain_own,
    gain_pair,
    gain_sibling,
    gain_chips,
    enc_dw,
    enc_sibling,
    enc_pair,
    enc_chips,
    dec_dw,
    dec_sibling,
    dec_pair,
    dec_chips,
    local_sem,
    quad_send,
    quad_sem,
    half_send,
    half_sem,
    fwd_sem,
    bwd_sem,
    skip_sem,
    scot_sem,
    dec_sem,
    grad_sem,
    owner_send,
    owner_sem,
    enc_send,
    dec_send,
    enc_pair_sem,
    enc_chip_sem,
    dec_pair_sem,
    dec_chip_sem,
    gain_pair_sem,
    gain_chip_sem,
):
    channels = noise_ref.shape[-1]
    count = 24 * (channels // GROUPS)
    own = lax.axis_index("section")
    last = sections - 1
    quad, member = own // 4, lax.rem(own, 4)
    quads = sections // 4
    dp = lax.axis_index("dp")
    p, c = dp // 2, lax.rem(dp, 2)
    sibling = dp + 1 - 2 * c
    across = 2 - 4 * lax.rem(p, 2)
    odd = lax.rem(own, 2)
    chips = enc_dw.shape[0]
    half_rows = dec_w.shape[1] // 2
    enc_sems = [enc_pair_sem.at[0], enc_pair_sem.at[1], enc_chip_sem.at[0], enc_chip_sem.at[1]]
    dec_sems = [dec_pair_sem.at[0], dec_pair_sem.at[1], dec_chip_sem.at[0], dec_chip_sem.at[1]]
    enc_bufs = [enc_dw, enc_sibling, enc_pair, enc_chips]
    dec_bufs = [dec_dw, dec_sibling, dec_pair, dec_chips]

    def remote(src, dst, send_sem, recv_sem, **device):
        return pltpu.make_async_remote_copy(
            src_ref=src,
            dst_ref=dst,
            send_sem=send_sem,
            recv_sem=recv_sem,
            device_id=device,
            device_id_type=MESH,
        )

    def at(section):
        return {"section": section, "dp": dp + across * lax.rem(section + own, 2)}

    def wait(ref, sem):
        pltpu.make_async_copy(ref, ref, sem).wait()

    load_enc = pltpu.make_async_copy(enc_hbm, enc_w, local_sem.at[0])
    load_dec = pltpu.make_async_copy(dec_hbm, dec_w.at[member], local_sem.at[1])
    load_enc.start()
    load_dec.start()
    gain_quad[member] = jnp.broadcast_to(dec_gain_ref[...], gain_quad.shape[1:])

    barrier = pltpu.get_barrier_semaphore()

    def greet(o, carry):
        pl.semaphore_signal(
            barrier,
            inc=1,
            device_id=at(lax.rem(own + o, sections)),
            device_id_type=MESH,
        )
        return carry

    lax.fori_loop(1, sections, greet, 0)
    pl.semaphore_signal(barrier, inc=1, device_id={"dp": sibling}, device_id_type=MESH)
    for o in range(1, chips):
        pl.semaphore_signal(
            barrier,
            inc=1,
            device_id={"dp": 2 * lax.rem(p + o, chips) + c},
            device_id_type=MESH,
        )
    pl.semaphore_wait(barrier, last + chips)

    @pl.when(own == 0)
    def _():
        for j in range(micros):
            fwd_in[j] = first_ref[j]

    @pl.when(odd == 1)
    def _():
        remote(keep_ref, keep_used, local_sem.at[2], local_sem.at[3], dp=dp + across).start()

        @pl.when(quad == quads - 1)
        def _():
            remote(noise_ref, noise_used, local_sem.at[4], local_sem.at[5], dp=dp + across).start()

        wait(keep_used, local_sem.at[3])

    @pl.when(odd == 0)
    def _():
        keep_used[...] = keep_ref[...]

        @pl.when(quad == quads - 1)
        def _():
            noise_used[...] = noise_ref[...]

    def kept_at(sample, level):
        row = keep_used[sample, pl.ds(level, 1), :]
        return jnp.concatenate([row] * (channels // row.shape[-1]), axis=1)

    half = pl.ds(pl.multiple_of(c * half_rows, half_rows), half_rows)
    other_half = pl.ds(pl.multiple_of((1 - c) * half_rows, half_rows), half_rows)

    def share(o, carry):
        to = 4 * quad + lax.rem(member + o, 4)
        remote(
            dec_hbm.at[half],
            dec_w.at[member, half],
            quad_send.at[0, o],
            quad_sem.at[0, member],
            **at(to),
        ).start()
        remote(
            gain_quad.at[member],
            gain_quad.at[member],
            quad_send.at[1, o],
            quad_sem.at[1, member],
            **at(to),
        ).start()
        return carry

    @pl.when(own >= sections // 2)
    def _():
        lax.fori_loop(1, 4, share, 0)

    dge_ref[...] = jnp.zeros_like(dge_ref)
    load_enc.wait()

    opposite = last - own
    opposite_quad, opposite_level = opposite // 4, lax.rem(opposite, 4)

    def enc_forward(j, carry):
        @pl.when(own > 0)
        def _():
            wait(fwd_in.at[j], fwd_sem.at[j])

        values = cube(fwd_in[j].astype(F32))
        keep = kept_at(j, own)
        normed, scale, z, gate = norm_forward(values, enc_gain_ref[...], mix_ref, count)
        act = z * gate
        columns = spatial_taps(act, 1)
        branch = uncube(jnp.dot(columns, enc_w[...], preferred_element_type=F32))
        enc_out[j] = flat(values + keep * branch)[0]

        @pl.when(own < last)
        def _():
            remote(
                enc_out.at[j], fwd_in.at[j], enc_send.at[0, j], fwd_sem.at[j], **at(own + 1)
            ).start()

        pair, side = j // 2, lax.rem(j, 2)

        @pl.when(own == last)
        def _():
            remote(
                enc_out.at[j], dec_in.at[side], enc_send.at[0, j], dec_sem.at[side], **at(pair)
            ).start()

        remote(
            enc_out.at[j],
            skip_in.at[opposite_level, side],
            enc_send.at[1, j],
            skip_sem.at[opposite_level, side],
            **at(4 * opposite_quad + pair),
        ).start()
        enc_normed[j] = normed[0]
        enc_scale[j] = scale[0]
        enc_slope[j] = (gate * (1.0 + z * (1.0 - gate)))[0]
        enc_act[pl.ds(pl.multiple_of(j * 32, 32), 32), :] = padded_rows(act)
        return carry

    lax.fori_loop(0, micros, enc_forward, 0)

    @pl.when(own < sections // 2)
    def _():
        lax.fori_loop(1, 4, share, 0)

    def turn_tap(tap, carry):
        rows = pl.ds(pl.multiple_of(tap * channels, channels), channels)
        enc_w[rows, :] = enc_w[rows, :].astype(F32).T.astype(BF16)
        return carry

    def pass_half(o, carry):
        of = lax.rem(member + o, 4)
        wait(dec_w.at[of, half], quad_sem.at[0, of])
        wait(gain_quad.at[of], quad_sem.at[1, of])
        remote(
            dec_w.at[of, half], dec_w.at[of, half], half_send.at[of], half_sem.at[of], dp=sibling
        ).start()
        return carry

    def take_half(o, carry):
        of = lax.rem(member + o, 4)
        wait(dec_w.at[of, other_half], half_sem.at[of])
        return carry

    load_dec.wait()
    lax.fori_loop(1, 4, pass_half, 0)
    lax.fori_loop(0, 9, turn_tap, 0)
    turned[...] = enc_act[...].astype(F32).T.astype(BF16)
    lax.fori_loop(1, 4, take_half, 0)

    mine = pl.ds(2 * member, 2)

    @pl.when(quad == 0)
    def _():
        for side in range(2):
            wait(dec_in.at[side], dec_sem.at[side])

    @pl.when(quad > 0)
    def _():
        wait(dec_in, dec_sem.at[2])

    def dec_keeps(level):
        return [
            kept_at(2 * member + side, sections + 4 * quad + level)
            for side in range(2)
        ]

    def to_owner(source, target, kind, level):
        @pl.when(level != member)
        def _():
            remote(
                source.at[level],
                target,
                owner_send.at[kind, level],
                owner_sem.at[kind, member],
                **at(4 * quad + level),
            ).start()

    def dec_forward(level, stream):
        for side in range(2):
            wait(skip_in.at[level, side], skip_sem.at[level, side])
        values = stream + cube(skip_in[level].astype(F32))
        normed, scale, z, gate = norm_forward(values, gain_quad[level], mix_ref, count)
        act = z * gate
        branch = uncube(
            jnp.dot(temporal_taps(act, 1), dec_w[level], preferred_element_type=F32)
        )
        result = (stream + gated(branch, dec_keeps(level))).astype(BF16).astype(F32)
        dec_normed[level] = normed
        dec_scale[level] = scale
        dec_slope[level] = gate * (1.0 + z * (1.0 - gate))
        act_out[level] = flat(act)
        to_owner(act_out, act_in.at[mine], 0, level)
        return result

    result = lax.fori_loop(0, 4, dec_forward, cube(dec_in[...].astype(F32)))

    def halves_left(o, carry):
        of = lax.rem(member + o, 4)
        wait(dec_w.at[of, half], half_send.at[of])
        return carry

    lax.fori_loop(1, 4, halves_left, 0)

    def turn_dec(tap, carry):
        level = tap // 3
        rows = pl.ds(pl.multiple_of(lax.rem(tap, 3) * channels, channels), channels)
        dec_w[level, rows, :] = dec_w[level, rows, :].astype(F32).T.astype(BF16)
        return carry

    @pl.when(quad < quads - 1)
    def _():
        dec_out[...] = flat(result)
        remote(dec_out, dec_in, dec_send.at[0], dec_sem.at[2], **at(own + 4)).start()
        lax.fori_loop(0, 12, turn_dec, 0)
        wait(grad_in, grad_sem)

    @pl.when(quad == quads - 1)
    def _():
        @pl.when(odd == 1)
        def _():
            wait(noise_used, local_sem.at[5])

        gap = result - cube(noise_used[mine].astype(F32))
        grad_in[...] = flat(gap * loss_scale)

    def dec_backward(step, upstream):
        level = 3 - step
        gate = gated(upstream, dec_keeps(level))
        h_out[level] = flat(gate)
        to_owner(h_out, h_in.at[mine], 1, level)
        columns = temporal_taps(gate, -1)

        @pl.when(quad < quads - 1)
        def _():
            product[...] = jnp.dot(columns, dec_w[level], preferred_element_type=F32)

        @pl.when(quad == quads - 1)
        def _():
            product[...] = transposed_product(columns, dec_w.at[level], channels)

        cot = uncube(product[...])
        grad, gain_part = norm_backward(
            cot,
            dec_normed[level],
            dec_scale[level],
            dec_slope[level],
            gain_quad[level],
            mix_ref,
            count,
        )
        s_out[level] = flat(grad)
        remote(
            s_out.at[level],
            scot_in.at[mine],
            dec_send.at[2 + level],
            scot_sem.at[member],
            **at(last - 4 * quad - level),
        ).start()
        part_out[level] = gain_part
        to_owner(part_out, part_in.at[member], 2, level)
        return (upstream + grad).astype(BF16).astype(F32)

    result = lax.fori_loop(0, 4, dec_backward, cube(grad_in[...].astype(F32)))
    grad_out[...] = flat(result)

    @pl.when(quad > 0)
    def _():
        remote(grad_out, grad_in, dec_send.at[1], grad_sem, **at(own - 4)).start()

    @pl.when(quad == 0)
    def _():
        remote(
            grad_out, bwd_in.at[mine], dec_send.at[1], bwd_sem.at[micros + member], **at(last)
        ).start()

    act_in[mine] = act_out[member]
    h_in[mine] = h_out[member]
    part_in[member] = part_out[member]

    def from_member(o, carry):
        of = lax.rem(member + o, 4)
        theirs = pl.ds(2 * of, 2)
        wait(act_in.at[theirs], owner_sem.at[0, of])
        wait(h_in.at[theirs], owner_sem.at[1, of])
        wait(part_in.at[of], owner_sem.at[2, of])
        return carry

    lax.fori_loop(1, 4, from_member, 0)

    def lay_out(j, carry):
        rows = pl.ds(pl.multiple_of(j * 32, 32), 32)
        dec_act[rows, :] = padded_rows(cube(act_in[j].astype(F32)))
        dec_cot[rows, :] = temporal_taps(cube(h_in[j].astype(F32)), -1)
        return carry

    lax.fori_loop(0, micros, lay_out, 0)
    weight_terms(dec_act[...].astype(F32).T.astype(BF16), dec_cot, dec_dw, channels)
    scatter_start(p, c, sibling, dec_bufs, dec_sems)

    def enc_backward(j, carry):
        @pl.when(lax.rem(j, 2) == 0)
        def _():
            pair = j // 2
            both = pl.ds(j, 2)
            wait(scot_in.at[both], scot_sem.at[pair])

            @pl.when(own == last)
            def _():
                wait(bwd_in.at[both], bwd_sem.at[micros + pair])

        @pl.when(own < last)
        def _():
            wait(bwd_in.at[j], bwd_sem.at[j])

        upstream = cube(
            (bwd_in[j].astype(F32) + scot_in[j].astype(F32)).astype(BF16).astype(F32)
        )
        keep = kept_at(j, own)
        columns = spatial_taps(keep * upstream, -1)
        cot = uncube(jnp.dot(columns, enc_w[...], preferred_element_type=F32))
        grad, gain_part = norm_backward(
            cot,
            enc_normed[j][None],
            enc_scale[j][None],
            enc_slope[j][None],
            enc_gain_ref[...],
            mix_ref,
            count,
        )

        @pl.when(own > 0)
        def _():
            q_out[j] = flat(upstream + grad)[0]
            remote(
                q_out.at[j], bwd_in.at[j], enc_send.at[2, j], bwd_sem.at[j], **at(own - 1)
            ).start()

        dge_ref[...] += gain_part
        enc_cot[pl.ds(pl.multiple_of(j * 32, 32), 32), :] = columns
        return carry

    lax.fori_loop(0, micros, enc_backward, 0)
    dgd = part_in[0] + part_in[1] + part_in[2] + part_in[3]
    row = lax.broadcasted_iota(jnp.int32, (8, channels), 0)
    gain_own[...] = jnp.where(
        row == 0,
        jnp.sum(dge_ref[...], axis=0, keepdims=True),
        jnp.where(row == 1, jnp.sum(dgd, axis=0, keepdims=True), 0.0),
    )
    to_pair = remote(
        gain_own, gain_sibling, gain_pair_sem.at[0], gain_pair_sem.at[1], dp=sibling
    )
    to_pair.start()
    weight_terms(turned[...], enc_cot, enc_dw, channels)
    scatter_start(p, c, sibling, enc_bufs, enc_sems)
    to_pair.wait()
    gain_pair[...] = gain_own[...] + gain_sibling[...]

    def gain_to_chip(o, carry):
        remote(
            gain_pair,
            gain_chips.at[o - 1],
            gain_chip_sem.at[0, o - 1],
            gain_chip_sem.at[1, o - 1],
            dp=2 * lax.rem(p + o, chips) + c,
        ).start()
        return carry

    lax.fori_loop(1, chips, gain_to_chip, 0)
    for step in range(2):
        scatter_step(p, c, dec_bufs, dec_sems, step)
        scatter_step(p, c, enc_bufs, enc_sems, step)
    scatter_end(p, c, dec_bufs, dec_sems, dwd_out)
    scatter_end(p, c, enc_bufs, enc_sems, dwe_out)

    def gain_arrived(o, carry):
        for side in range(2):
            wait(gain_chips.at[o], gain_chip_sem.at[side, o])
        return carry

    lax.fori_loop(0, chips - 1, gain_arrived, 0)
    total = gain_pair[...]
    for o in range(chips - 1):
        total = total + gain_chips[o]
    gain_out[...] = total

    def drain(j, carry):
        for kind in range(2):
            wait(enc_out.at[j], enc_send.at[kind, j])

        @pl.when(own > 0)
        def _():
            wait(q_out.at[j], enc_send.at[2, j])

        return carry

    def drain_quad(o, carry):
        of = lax.rem(member + o, 4)
        wait(dec_w.at[of, half], quad_send.at[0, o])
        wait(gain_quad.at[of], quad_send.at[1, o])
        wait(act_out.at[of], owner_send.at[0, of])
        wait(h_out.at[of], owner_send.at[1, of])
        wait(part_out.at[of], owner_send.at[2, of])
        return carry

    def drain_scot(level, carry):
        wait(s_out.at[level], dec_send.at[2 + level])
        return carry

    lax.fori_loop(0, micros, drain, 0)
    lax.fori_loop(1, 4, drain_quad, 0)
    lax.fori_loop(0, 4, drain_scot, 0)
    wait(grad_out, dec_send.at[1])

    @pl.when(quad < quads - 1)
    def _():
        wait(dec_out, dec_send.at[0])

    @pl.when(odd == 1)
    def _():
        wait(keep_used, local_sem.at[2])

        @pl.when(quad == quads - 1)
        def _():
            wait(noise_used, local_sem.at[4])


def body(
    clip_pool,
    sample_ids,
    timesteps,
    noise_draw,
    keep_lists,
    enc_weight,
    enc_gain,
    dec_weight,
    dec_gain,
):
    sections = lax.axis_size("section")
    micros = noise_draw.shape[0]
    channels = noise_draw.shape[-1]
    positions = noise_draw.shape[1] * noise_draw.shape[2] * noise_draw.shape[3]
    scale = 1.0 / math.sqrt(micros * lax.axis_size("dp") * positions)
    lined = (micros, positions, channels)
    noise = noise_draw.reshape(lined)
    clips = clip_pool.reshape((-1,) + lined[1:])
    clean = jnp.zeros(lined, F32)
    for clip in range(clips.shape[0]):
        clean = jnp.where((sample_ids == clip)[:, None, None], clips[clip][None].astype(F32), clean)
    level = noise_level(timesteps)[:, None, None]
    first = (jnp.sqrt(level) * clean + jnp.sqrt(1.0 - level) * noise.astype(F32)).astype(BF16)
    keeps = jnp.broadcast_to(keep_lists.astype(F32)[:, :, None], keep_lists.shape + (128,))
    member = np.arange(channels) // (channels // GROUPS)
    mix = jnp.asarray((member[:, None] == member[None, :]).astype(np.float32), BF16)
    vmem = pl.BlockSpec(memory_space=pltpu.VMEM)
    hbm = pl.BlockSpec(memory_space=pl.ANY)
    slots = lambda *lead: pltpu.VMEM(lead + (positions, channels), BF16)
    kept = lambda *lead: pltpu.VMEM(lead + (3, 8, channels), F32)
    rows = 32 * micros
    group = lax.axis_size("dp")
    chips = group // 2
    wide = lambda *lead: pltpu.VMEM(lead + (40, channels), BF16)
    enc_blocks, dec_blocks = 9 * channels // group // 40, 3 * channels // group // 40
    shares = lambda n: [wide(chips, 2, n), wide(chips, n), wide(chips, n), wide(chips - 1, n)]
    dwe, dwd, gains = pl.pallas_call(
        lambda *refs: pipeline_kernel(sections, micros, scale, *refs),
        out_shape=(
            jax.ShapeDtypeStruct((enc_blocks, 40, channels), F32),
            jax.ShapeDtypeStruct((dec_blocks, 40, channels), F32),
            jax.ShapeDtypeStruct((8, channels), F32),
        ),
        in_specs=[vmem, vmem, vmem, vmem, vmem, vmem, hbm, hbm],
        out_specs=(vmem, vmem, vmem),
        scratch_shapes=[
            pltpu.VMEM((9 * channels, channels), BF16),
            pltpu.VMEM((4, 3 * channels, channels), BF16),
            pltpu.VMEM((micros, 2 * sections, 128), F32),
            slots(micros),
            pltpu.VMEM((4, 8, channels), F32),
            slots(micros),
            slots(micros),
            slots(4, 2),
            slots(micros),
            slots(2),
            slots(2),
            slots(micros),
            slots(2),
            slots(2),
            slots(4, 2),
            slots(micros),
            kept(micros),
            kept(micros),
            pltpu.VMEM((micros, 8, channels), F32),
            pltpu.VMEM((rows, channels), BF16),
            pltpu.VMEM((rows, 9 * channels), BF16),
            kept(4, 2),
            kept(4, 2),
            pltpu.VMEM((4, 2, 8, channels), F32),
            slots(4, 2),
            slots(4, 2),
            pltpu.VMEM((4, 8, channels), F32),
            slots(micros),
            slots(micros),
            pltpu.VMEM((4, 8, channels), F32),
            pltpu.VMEM((rows, channels), BF16),
            pltpu.VMEM((rows, 3 * channels), BF16),
            pltpu.VMEM((64, channels), F32),
            pltpu.VMEM((channels, rows), BF16),
            pltpu.VMEM((8, channels), F32),
            pltpu.VMEM((8, channels), F32),
            pltpu.VMEM((8, channels), F32),
            pltpu.VMEM((8, channels), F32),
            pltpu.VMEM((chips - 1, 8, channels), F32),
            *shares(enc_blocks),
            *shares(dec_blocks),
            pltpu.SemaphoreType.DMA((6,)),
            pltpu.SemaphoreType.DMA((2, 4)),
            pltpu.SemaphoreType.DMA((2, 4)),
            pltpu.SemaphoreType.DMA((4,)),
            pltpu.SemaphoreType.DMA((4,)),
            pltpu.SemaphoreType.DMA((micros,)),
            pltpu.SemaphoreType.DMA((micros + 4,)),
            pltpu.SemaphoreType.DMA((4, 2)),
            pltpu.SemaphoreType.DMA((4,)),
            pltpu.SemaphoreType.DMA((3,)),
            pltpu.SemaphoreType.DMA,
            pltpu.SemaphoreType.DMA((3, 4)),
            pltpu.SemaphoreType.DMA((3, 4)),
            pltpu.SemaphoreType.DMA((3, micros)),
            pltpu.SemaphoreType.DMA((6,)),
            pltpu.SemaphoreType.DMA((2, chips)),
            pltpu.SemaphoreType.DMA((2, 3, chips - 1)),
            pltpu.SemaphoreType.DMA((2, chips)),
            pltpu.SemaphoreType.DMA((2, 3, chips - 1)),
            pltpu.SemaphoreType.DMA((2,)),
            pltpu.SemaphoreType.DMA((2, chips - 1)),
        ],
        compiler_params=pltpu.CompilerParams(
            collective_id=0, has_side_effects=True, vmem_limit_bytes=60 << 20
        ),
        name="pipeline",
    )(keeps, first, noise, enc_gain, dec_gain, mix, enc_weight[0], dec_weight[0])
    part = channels // group
    gains = lax.dynamic_slice_in_dim(gains, lax.axis_index("dp") * part, part, 1)
    return (
        dwe.reshape(1, -1, channels),
        gains[0:1],
        dwd.reshape(1, -1, channels),
        gains[1:2],
    )


def solution(mesh):
    placed = (
        P("dp", None, None, None, None),
        P("dp"),
        P("dp"),
        P("dp", None, None, None, None),
        P("dp", None),
        P("section", None, None),
        P("section", None),
        P("section", None, None),
        P("section", None),
    )
    return jax.shard_map(
        body,
        mesh=mesh,
        in_specs=placed,
        out_specs=(
            P("section", "dp", None),
            P("section", "dp"),
            P("section", "dp", None),
            P("section", "dp"),
        ),
        check_vma=False,
    )
```

```python
import math

import jax
import jax.numpy as jnp
import numpy as np
from jax import lax
from jax.experimental import pallas as pl
from jax.experimental.pallas import tpu as pltpu
from jax.sharding import PartitionSpec as P

GROUPS = 32
F32, BF16 = jnp.float32, jnp.bfloat16
MESH = pl.DeviceIdType.MESH


def noise_level(timesteps):
    phase_arg = (timesteps.astype(F32) / 1000.0 + 0.008) / 1.008
    return jnp.cos(phase_arg * (math.pi / 2.0)) ** 2


def over_rows(values):
    part = values[:, 0] + values[:, 1] + values[:, 2]
    return jnp.broadcast_to(jnp.sum(part, axis=1, keepdims=True), part.shape)


def split_terms(values):
    high = values.astype(BF16).astype(F32)
    rest = values - high
    middle = rest.astype(BF16).astype(F32)
    return [high, middle, rest - middle]


def group_means(sums, mix_ref, count):
    terms = [term for each in sums for term in split_terms(each)]
    stacked = jnp.concatenate(terms, axis=0)
    samples, rows, channels = sums[0].shape
    mixed = jnp.dot(
        stacked.reshape(-1, channels).astype(BF16), mix_ref[...], preferred_element_type=F32
    ).reshape(-1, samples, rows, channels)
    return [
        (mixed[3 * i] + mixed[3 * i + 1] + mixed[3 * i + 2]) * (1.0 / count)
        for i in range(len(sums))
    ]


def cube(values):
    return values.reshape(-1, 3, 8, values.shape[-1])


def uncube(product):
    return product.reshape(-1, 4, 8, product.shape[-1])[:, :3]


def flat(values):
    return values.reshape(-1, 24, values.shape[-1]).astype(BF16)


def padded_rows(values):
    full = jnp.concatenate([values, jnp.zeros_like(values[:, :1])], axis=1)
    return full.reshape(-1, values.shape[-1]).astype(BF16)


def spatial_taps(values, sign):
    place = lax.broadcasted_iota(jnp.int32, values.shape, 2)
    high, wide = place // 2, place % 2
    taps = []
    for tap in range(9):
        down, across = sign * (tap // 3 - 1), sign * (tap % 3 - 1)
        shift = 2 * down + across
        moved = pltpu.roll(values, (-shift) % 8, 2) if shift % 8 else values
        if down or across:
            inside = (
                (high + down >= 0) & (high + down < 4) & (wide + across >= 0) & (wide + across < 2)
            )
            moved = jnp.where(inside, moved, 0.0)
        taps.append(padded_rows(moved))
    return jnp.concatenate(taps, axis=1)


def temporal_taps(values, sign):
    zero = jnp.zeros_like(values[:, :1])
    before = jnp.concatenate([zero, values[:, :2]], axis=1)
    after = jnp.concatenate([values[:, 1:], zero], axis=1)
    taps = [before, values, after] if sign > 0 else [after, values, before]
    return jnp.concatenate([padded_rows(tap) for tap in taps], axis=1)


def norm_forward(values, gain, mix_ref, count):
    mean, square = group_means([over_rows(values), over_rows(values * values)], mix_ref, count)
    spread = jnp.maximum(square - mean * mean, 0.0)
    center = values - mean[:, None]
    scale = lax.rsqrt(spread + 1e-05)
    normed = center * scale[:, None]
    z = normed * gain[None, None]
    gate = 1.0 / (1.0 + jnp.exp(-z))
    return normed, scale, z, gate


def norm_backward(cot, normed, scale, slope, gain, mix_ref, count):
    dz = cot * slope
    gain_part = dz * normed
    gain_part = jnp.sum(gain_part[:, 0] + gain_part[:, 1] + gain_part[:, 2], axis=0)
    dn = dz * gain[None, None]
    mean_dn, mean_dnn = group_means([over_rows(dn), over_rows(dn * normed)], mix_ref, count)
    grad = scale[:, None] * (dn - mean_dn[:, None] - normed * mean_dnn[:, None])
    return grad, gain_part


def gated(values, keeps):
    return jnp.concatenate([values[s : s + 1] * keep for s, keep in enumerate(keeps)], axis=0)


def transposed_product(columns, weight_ref, channels):
    total = None
    for at in range(0, columns.shape[1], channels):
        part = lax.dot_general(
            columns[:, at : at + channels],
            weight_ref[at : at + channels, :],
            (((1,), (1,)), ((), ())),
            preferred_element_type=F32,
        )
        total = part if total is None else total + part
    return total


def halving(p):
    y, x = p // 2, lax.rem(p, 2)
    ring = lambda row: lax.rem((row + 1) // 2, 2)
    side, half = ring(y), y // 2
    next_y = y + 1 - 2 * lax.rem(y, 2)
    far_y = 3 - y
    row = lambda which, i: which + i * (3 - 2 * which)
    over_x, over_a, over_b = 2 * y + 1 - x, 2 * next_y + x, 2 * far_y + x
    return [
        dict(
            partners=[over_x, over_a, over_b],
            kept=[lambda i: 2 * i + x, lambda i: 2 * row(side, i) + x],
            sent=lambda i: 2 * row(1 - side, i) + x,
            goes=lambda m: (lax.rem(m, 2) != x, m // 2),
        ),
        dict(
            partners=[over_a, over_b, over_x],
            kept=[lambda i: 2 * row(side, i // 2) + lax.rem(i, 2), lambda i: 2 * y + i],
            sent=lambda i: 2 * far_y + i,
            goes=lambda m: (ring(m // 2) != side, 2 * (m // 4) + lax.rem(m, 2)),
        ),
        dict(
            partners=[over_b, over_x, over_a],
            kept=[lambda i: 4 * half + i, lambda i: 2 * (2 * half + i) + x],
            sent=lambda i: 2 * (2 * half + i) + 1 - x,
            goes=lambda m: (m // 4 != half, lax.rem(m, 4)),
        ),
    ]


def chip_copy(c, third, src, place, buffers, sems, partner):
    _, _, pair, from_chips = buffers
    width = pair.shape[1] // 3
    blocks = pl.ds(third * width, width)
    return pltpu.make_async_remote_copy(
        src_ref=pair.at[src, blocks],
        dst_ref=from_chips.at[place, blocks],
        send_sem=sems[2].at[third, place],
        recv_sem=sems[3].at[third, place],
        device_id={"dp": 2 * partner + c},
        device_id_type=MESH,
    )


def wait_third(from_chips, third, place, sem):
    width = from_chips.shape[1] // 3
    ref = from_chips.at[place, pl.ds(third * width, width)]
    pltpu.make_async_copy(ref, ref, sem.at[third, place]).wait()


def scatter_start(p, c, buffers, sems):
    dw, from_sibling, pair, from_chips = buffers
    chips = dw.shape[0]
    arrive_pair = sems[1]
    orders = halving(p)

    def add_pair(m, carry):
        pltpu.make_async_copy(from_sibling.at[m], from_sibling.at[m], arrive_pair.at[m]).wait()

        def add(block, inner):
            pair[m, block] = (
                dw[m, c, block].astype(F32) + from_sibling[m, block].astype(F32)
            ).astype(BF16)
            return inner

        lax.fori_loop(0, dw.shape[2], add, 0)
        for third, order in enumerate(orders):
            goes, place = order["goes"](m)

            @pl.when(goes)
            def _():
                chip_copy(c, third, m, place, buffers, sems, order["partners"][0]).start()

        return carry

    lax.fori_loop(0, chips, add_pair, 0)


def scatter_step(p, c, buffers, sems, step):
    _, _, pair, from_chips = buffers
    width = pair.shape[1] // 3
    base = 4 * step
    for third, order in enumerate(halving(p)):

        def take(i, carry):
            wait_third(from_chips, third, base + i, sems[3])
            kept = order["kept"][step](i)

            def add(n, inner):
                block = third * width + n
                pair[kept, block] = (
                    pair[kept, block].astype(F32) + from_chips[base + i, block].astype(F32)
                ).astype(BF16)
                return inner

            lax.fori_loop(0, width, add, 0)
            return carry

        lax.fori_loop(0, 4 if step == 0 else 2, take, 0)
        if step == 0:
            for i in range(2):
                chip_copy(
                    c, third, order["sent"](i), 4 + i, buffers, sems, order["partners"][1]
                ).start()
        else:
            partner = order["partners"][2]
            chip_copy(c, third, partner, 6, buffers, sems, partner).start()


def scatter_end(p, c, buffers, sems, out_ref):
    _, from_sibling, pair, from_chips = buffers
    chips = pair.shape[0]
    width = pair.shape[1] // 3
    for third in range(3):
        wait_third(from_chips, third, 6, sems[3])

        def add(n, carry):
            block = third * width + n
            out_ref[block] = pair[p, block].astype(F32) + from_chips[6, block].astype(F32)
            return carry

        lax.fori_loop(0, width, add, 0)

    def sent(place, carry):
        for third in range(3):
            wait_third(from_chips, third, place, sems[2])
        return carry

    def sent_pair(m, carry):
        pltpu.make_async_copy(from_sibling.at[m], from_sibling.at[m], sems[0].at[m]).wait()
        return carry

    lax.fori_loop(0, chips - 1, sent, 0)
    lax.fori_loop(0, chips, sent_pair, 0)


def weight_terms(turned, cot, c, sibling, buffers, sems, channels):
    dw, from_sibling, _, _ = buffers
    blocks = dw.shape[2]
    per_tap = channels // 40
    gone = 0
    for tap in range(cot.shape[1] // channels):
        part = jnp.dot(
            turned,
            cot[:, tap * channels : (tap + 1) * channels],
            preferred_element_type=F32,
        ).reshape(per_tap, 40, channels)
        for i in range(per_tap):
            at = tap * per_tap + i
            dw[at // (2 * blocks), (at // blocks) % 2, at % blocks] = part[i].astype(BF16)
        ready = (tap + 1) * per_tap // (2 * blocks)

        def to_sibling(m, carry):
            pltpu.make_async_remote_copy(
                src_ref=dw.at[m, 1 - c],
                dst_ref=from_sibling.at[m],
                send_sem=sems[0].at[m],
                recv_sem=sems[1].at[m],
                device_id={"dp": sibling},
                device_id_type=MESH,
            ).start()
            return carry

        lax.fori_loop(gone, ready, to_sibling, 0)
        gone = ready


def pipeline_kernel(
    sections,
    micros,
    loss_scale,
    keep_ref,
    first_ref,
    noise_ref,
    enc_gain_ref,
    dec_gain_ref,
    mix_ref,
    enc_hbm,
    dec_hbm,
    dwe_out,
    dwd_out,
    gain_out,
    enc_w,
    dec_w,
    keep_used,
    noise_used,
    gain_quad,
    fwd_in,
    bwd_in,
    skip_in,
    scot_in,
    dec_in,
    grad_in,
    enc_out,
    dec_out,
    grad_out,
    s_out,
    q_out,
    enc_normed,
    enc_slope,
    enc_scale,
    enc_act,
    enc_cot,
    dec_normed,
    dec_slope,
    dec_scale,
    act_out,
    h_out,
    part_out,
    act_in,
    h_in,
    part_in,
    dec_act,
    dec_cot,
    product,
    turned,
    dge_ref,
    gain_own,
    gain_pair,
    gain_sibling,
    gain_chips,
    enc_dw,
    enc_sibling,
    enc_pair,
    enc_chips,
    dec_dw,
    dec_sibling,
    dec_pair,
    dec_chips,
    local_sem,
    quad_send,
    quad_sem,
    half_send,
    half_sem,
    fwd_sem,
    bwd_sem,
    skip_sem,
    scot_sem,
    dec_sem,
    grad_sem,
    owner_send,
    owner_sem,
    enc_send,
    dec_send,
    enc_pair_sem,
    enc_chip_sem,
    dec_pair_sem,
    dec_chip_sem,
    gain_pair_sem,
    gain_chip_sem,
):
    channels = noise_ref.shape[-1]
    count = 24 * (channels // GROUPS)
    own = lax.axis_index("section")
    last = sections - 1
    quad, member = own // 4, lax.rem(own, 4)
    quads = sections // 4
    dp = lax.axis_index("dp")
    p, c = dp // 2, lax.rem(dp, 2)
    sibling = dp + 1 - 2 * c
    across = 2 - 4 * lax.rem(p, 2)
    odd = lax.rem(own, 2)
    chips = enc_dw.shape[0]
    half_rows = dec_w.shape[1] // 2
    enc_sems = [enc_pair_sem.at[0], enc_pair_sem.at[1], enc_chip_sem.at[0], enc_chip_sem.at[1]]
    dec_sems = [dec_pair_sem.at[0], dec_pair_sem.at[1], dec_chip_sem.at[0], dec_chip_sem.at[1]]
    enc_bufs = [enc_dw, enc_sibling, enc_pair, enc_chips]
    dec_bufs = [dec_dw, dec_sibling, dec_pair, dec_chips]

    def remote(src, dst, send_sem, recv_sem, **device):
        return pltpu.make_async_remote_copy(
            src_ref=src,
            dst_ref=dst,
            send_sem=send_sem,
            recv_sem=recv_sem,
            device_id=device,
            device_id_type=MESH,
        )

    def at(section):
        return {"section": section, "dp": dp + across * lax.rem(section + own, 2)}

    def wait(ref, sem):
        pltpu.make_async_copy(ref, ref, sem).wait()

    load_enc = pltpu.make_async_copy(enc_hbm, enc_w, local_sem.at[0])
    load_dec = pltpu.make_async_copy(dec_hbm, dec_w.at[member], local_sem.at[1])
    load_enc.start()
    load_dec.start()
    gain_quad[member] = jnp.broadcast_to(dec_gain_ref[...], gain_quad.shape[1:])

    barrier = pltpu.get_barrier_semaphore()

    def greet(o, carry):
        pl.semaphore_signal(
            barrier,
            inc=1,
            device_id=at(lax.rem(own + o, sections)),
            device_id_type=MESH,
        )
        return carry

    lax.fori_loop(1, sections, greet, 0)
    pl.semaphore_signal(barrier, inc=1, device_id={"dp": sibling}, device_id_type=MESH)
    for o in range(1, chips):
        pl.semaphore_signal(
            barrier,
            inc=1,
            device_id={"dp": 2 * lax.rem(p + o, chips) + c},
            device_id_type=MESH,
        )
    pl.semaphore_wait(barrier, last + chips)

    @pl.when(own == 0)
    def _():
        for j in range(micros):
            fwd_in[j] = first_ref[j]

    @pl.when(odd == 1)
    def _():
        remote(keep_ref, keep_used, local_sem.at[2], local_sem.at[3], dp=dp + across).start()

        @pl.when(quad == quads - 1)
        def _():
            remote(noise_ref, noise_used, local_sem.at[4], local_sem.at[5], dp=dp + across).start()

        wait(keep_used, local_sem.at[3])

    @pl.when(odd == 0)
    def _():
        keep_used[...] = keep_ref[...]

        @pl.when(quad == quads - 1)
        def _():
            noise_used[...] = noise_ref[...]

    def kept_at(sample, level):
        row = keep_used[sample, pl.ds(level, 1), :]
        return jnp.concatenate([row] * (channels // row.shape[-1]), axis=1)

    half = pl.ds(pl.multiple_of(c * half_rows, half_rows), half_rows)
    other_half = pl.ds(pl.multiple_of((1 - c) * half_rows, half_rows), half_rows)

    def share(o, carry):
        to = 4 * quad + lax.rem(member + o, 4)
        remote(
            dec_hbm.at[half],
            dec_w.at[member, half],
            quad_send.at[0, o],
            quad_sem.at[0, member],
            **at(to),
        ).start()
        remote(
            gain_quad.at[member],
            gain_quad.at[member],
            quad_send.at[1, o],
            quad_sem.at[1, member],
            **at(to),
        ).start()
        return carry

    @pl.when(own >= sections // 2)
    def _():
        lax.fori_loop(1, 4, share, 0)

    dge_ref[...] = jnp.zeros_like(dge_ref)

    opposite = last - own
    opposite_quad, opposite_level = opposite // 4, lax.rem(opposite, 4)

    def enc_forward(j, carry):
        @pl.when(own > 0)
        def _():
            wait(fwd_in.at[j], fwd_sem.at[j])

        values = cube(fwd_in[j].astype(F32))
        keep = kept_at(j, own)
        normed, scale, z, gate = norm_forward(values, enc_gain_ref[...], mix_ref, count)
        act = z * gate
        columns = spatial_taps(act, 1)

        @pl.when(j == 0)
        def _():
            load_enc.wait()

        branch = uncube(jnp.dot(columns, enc_w[...], preferred_element_type=F32))
        enc_out[j] = flat(values + keep * branch)[0]

        @pl.when(own < last)
        def _():
            remote(
                enc_out.at[j], fwd_in.at[j], enc_send.at[0, j], fwd_sem.at[j], **at(own + 1)
            ).start()

        pair, side = j // 2, lax.rem(j, 2)

        @pl.when(own == last)
        def _():
            remote(
                enc_out.at[j], dec_in.at[side], enc_send.at[0, j], dec_sem.at[side], **at(pair)
            ).start()

        remote(
            enc_out.at[j],
            skip_in.at[opposite_level, side],
            enc_send.at[1, j],
            skip_sem.at[opposite_level, side],
            **at(4 * opposite_quad + pair),
        ).start()
        enc_normed[j] = normed[0]
        enc_scale[j] = scale[0]
        enc_slope[j] = (gate * (1.0 + z * (1.0 - gate)))[0]
        enc_act[pl.ds(pl.multiple_of(j * 32, 32), 32), :] = padded_rows(act)
        return carry

    lax.fori_loop(0, micros, enc_forward, 0)

    @pl.when(own < sections // 2)
    def _():
        lax.fori_loop(1, 4, share, 0)

    def turn_tap(tap, carry):
        rows = pl.ds(pl.multiple_of(tap * channels, channels), channels)
        enc_w[rows, :] = enc_w[rows, :].astype(F32).T.astype(BF16)
        return carry

    def pass_half(o, carry):
        of = lax.rem(member + o, 4)
        wait(dec_w.at[of, half], quad_sem.at[0, of])
        wait(gain_quad.at[of], quad_sem.at[1, of])
        remote(
            dec_w.at[of, half], dec_w.at[of, half], half_send.at[of], half_sem.at[of], dp=sibling
        ).start()
        return carry

    def take_half(o, carry):
        of = lax.rem(member + o, 4)
        wait(dec_w.at[of, other_half], half_sem.at[of])
        return carry

    lax.fori_loop(0, 9, turn_tap, 0)
    turned[...] = enc_act[...].astype(F32).T.astype(BF16)
    load_dec.wait()
    lax.fori_loop(1, 4, pass_half, 0)
    lax.fori_loop(1, 4, take_half, 0)

    mine = pl.ds(2 * member, 2)

    @pl.when(quad == 0)
    def _():
        for side in range(2):
            wait(dec_in.at[side], dec_sem.at[side])

    @pl.when(quad > 0)
    def _():
        wait(dec_in, dec_sem.at[2])

    def dec_keeps(level):
        return [
            kept_at(2 * member + side, sections + 4 * quad + level)
            for side in range(2)
        ]

    def to_owner(source, target, kind, level):
        @pl.when(level != member)
        def _():
            remote(
                source.at[level],
                target,
                owner_send.at[kind, level],
                owner_sem.at[kind, member],
                **at(4 * quad + level),
            ).start()

    def dec_forward(level, stream):
        for side in range(2):
            wait(skip_in.at[level, side], skip_sem.at[level, side])
        values = stream + cube(skip_in[level].astype(F32))
        normed, scale, z, gate = norm_forward(values, gain_quad[level], mix_ref, count)
        act = z * gate
        branch = uncube(
            jnp.dot(temporal_taps(act, 1), dec_w[level], preferred_element_type=F32)
        )
        result = (stream + gated(branch, dec_keeps(level))).astype(BF16).astype(F32)
        dec_normed[level] = normed
        dec_scale[level] = scale
        dec_slope[level] = gate * (1.0 + z * (1.0 - gate))
        act_out[level] = flat(act)
        return result

    result = lax.fori_loop(0, 4, dec_forward, cube(dec_in[...].astype(F32)))

    def halves_left(o, carry):
        of = lax.rem(member + o, 4)
        wait(dec_w.at[of, half], half_send.at[of])
        return carry

    lax.fori_loop(1, 4, halves_left, 0)

    def turn_dec(tap, carry):
        level = tap // 3
        rows = pl.ds(pl.multiple_of(lax.rem(tap, 3) * channels, channels), channels)
        dec_w[level, rows, :] = dec_w[level, rows, :].astype(F32).T.astype(BF16)
        return carry

    @pl.when(quad < quads - 1)
    def _():
        dec_out[...] = flat(result)
        remote(dec_out, dec_in, dec_send.at[0], dec_sem.at[2], **at(own + 4)).start()
        lax.fori_loop(0, 12, turn_dec, 0)
        wait(grad_in, grad_sem)

    @pl.when(quad == quads - 1)
    def _():
        @pl.when(odd == 1)
        def _():
            wait(noise_used, local_sem.at[5])

        gap = result - cube(noise_used[mine].astype(F32))
        grad_in[...] = flat(gap * loss_scale)

    def dec_backward(step, upstream):
        level = 3 - step
        gate = gated(upstream, dec_keeps(level))
        h_out[level] = flat(gate)
        columns = temporal_taps(gate, -1)

        @pl.when(quad < quads - 1)
        def _():
            product[...] = jnp.dot(columns, dec_w[level], preferred_element_type=F32)

        @pl.when(quad == quads - 1)
        def _():
            product[...] = transposed_product(columns, dec_w.at[level], channels)

        cot = uncube(product[...])
        grad, gain_part = norm_backward(
            cot,
            dec_normed[level],
            dec_scale[level],
            dec_slope[level],
            gain_quad[level],
            mix_ref,
            count,
        )
        s_out[level] = flat(grad)
        part_out[level] = gain_part
        return (upstream + grad).astype(BF16).astype(F32)

    result = lax.fori_loop(0, 4, dec_backward, cube(grad_in[...].astype(F32)))
    grad_out[...] = flat(result)

    @pl.when(quad > 0)
    def _():
        remote(grad_out, grad_in, dec_send.at[1], grad_sem, **at(own - 4)).start()

    @pl.when(quad == 0)
    def _():
        remote(
            grad_out, bwd_in.at[mine], dec_send.at[1], bwd_sem.at[micros + member], **at(last)
        ).start()

    def hand_over(step, carry):
        level = 3 - step
        remote(
            s_out.at[level],
            scot_in.at[mine],
            dec_send.at[2 + level],
            scot_sem.at[member],
            **at(last - 4 * quad - level),
        ).start()
        to_owner(act_out, act_in.at[mine], 0, level)
        to_owner(h_out, h_in.at[mine], 1, level)
        to_owner(part_out, part_in.at[member], 2, level)
        return carry

    lax.fori_loop(0, 4, hand_over, 0)

    act_in[mine] = act_out[member]
    h_in[mine] = h_out[member]
    part_in[member] = part_out[member]

    def from_member(o, carry):
        of = lax.rem(member + o, 4)
        theirs = pl.ds(2 * of, 2)
        wait(act_in.at[theirs], owner_sem.at[0, of])
        wait(h_in.at[theirs], owner_sem.at[1, of])
        wait(part_in.at[of], owner_sem.at[2, of])
        return carry

    lax.fori_loop(1, 4, from_member, 0)

    def lay_out(j, carry):
        rows = pl.ds(pl.multiple_of(j * 32, 32), 32)
        dec_act[rows, :] = padded_rows(cube(act_in[j].astype(F32)))
        dec_cot[rows, :] = temporal_taps(cube(h_in[j].astype(F32)), -1)
        return carry

    lax.fori_loop(0, micros, lay_out, 0)
    weight_terms(
        dec_act[...].astype(F32).T.astype(BF16), dec_cot, c, sibling, dec_bufs, dec_sems, channels
    )
    scatter_start(p, c, dec_bufs, dec_sems)

    def enc_backward(j, carry):
        @pl.when(lax.rem(j, 2) == 0)
        def _():
            pair = j // 2
            both = pl.ds(j, 2)
            wait(scot_in.at[both], scot_sem.at[pair])

            @pl.when(own == last)
            def _():
                wait(bwd_in.at[both], bwd_sem.at[micros + pair])

        @pl.when(own < last)
        def _():
            wait(bwd_in.at[j], bwd_sem.at[j])

        upstream = cube(
            (bwd_in[j].astype(F32) + scot_in[j].astype(F32)).astype(BF16).astype(F32)
        )
        keep = kept_at(j, own)
        columns = spatial_taps(keep * upstream, -1)
        cot = uncube(jnp.dot(columns, enc_w[...], preferred_element_type=F32))
        grad, gain_part = norm_backward(
            cot,
            enc_normed[j][None],
            enc_scale[j][None],
            enc_slope[j][None],
            enc_gain_ref[...],
            mix_ref,
            count,
        )

        @pl.when(own > 0)
        def _():
            q_out[j] = flat(upstream + grad)[0]
            remote(
                q_out.at[j], bwd_in.at[j], enc_send.at[2, j], bwd_sem.at[j], **at(own - 1)
            ).start()

        dge_ref[...] += gain_part
        enc_cot[pl.ds(pl.multiple_of(j * 32, 32), 32), :] = columns
        return carry

    lax.fori_loop(0, micros, enc_backward, 0)
    dgd = part_in[0] + part_in[1] + part_in[2] + part_in[3]
    row = lax.broadcasted_iota(jnp.int32, (8, channels), 0)
    gain_own[...] = jnp.where(
        row == 0,
        jnp.sum(dge_ref[...], axis=0, keepdims=True),
        jnp.where(row == 1, jnp.sum(dgd, axis=0, keepdims=True), 0.0),
    )
    to_pair = remote(
        gain_own, gain_sibling, gain_pair_sem.at[0], gain_pair_sem.at[1], dp=sibling
    )
    to_pair.start()
    weight_terms(turned[...], enc_cot, c, sibling, enc_bufs, enc_sems, channels)
    scatter_start(p, c, enc_bufs, enc_sems)
    to_pair.wait()
    gain_pair[...] = gain_own[...] + gain_sibling[...]

    def gain_to_chip(o, carry):
        remote(
            gain_pair,
            gain_chips.at[o - 1],
            gain_chip_sem.at[0, o - 1],
            gain_chip_sem.at[1, o - 1],
            dp=2 * lax.rem(p + o, chips) + c,
        ).start()
        return carry

    lax.fori_loop(1, chips, gain_to_chip, 0)
    for step in range(2):
        scatter_step(p, c, dec_bufs, dec_sems, step)
        scatter_step(p, c, enc_bufs, enc_sems, step)
    scatter_end(p, c, dec_bufs, dec_sems, dwd_out)
    scatter_end(p, c, enc_bufs, enc_sems, dwe_out)

    def gain_arrived(o, carry):
        for side in range(2):
            wait(gain_chips.at[o], gain_chip_sem.at[side, o])
        return carry

    lax.fori_loop(0, chips - 1, gain_arrived, 0)
    total = gain_pair[...]
    for o in range(chips - 1):
        total = total + gain_chips[o]
    gain_out[...] = total

    def drain(j, carry):
        for kind in range(2):
            wait(enc_out.at[j], enc_send.at[kind, j])

        @pl.when(own > 0)
        def _():
            wait(q_out.at[j], enc_send.at[2, j])

        return carry

    def drain_quad(o, carry):
        of = lax.rem(member + o, 4)
        wait(dec_w.at[of, half], quad_send.at[0, o])
        wait(gain_quad.at[of], quad_send.at[1, o])
        wait(act_out.at[of], owner_send.at[0, of])
        wait(h_out.at[of], owner_send.at[1, of])
        wait(part_out.at[of], owner_send.at[2, of])
        return carry

    def drain_scot(level, carry):
        wait(s_out.at[level], dec_send.at[2 + level])
        return carry

    lax.fori_loop(0, micros, drain, 0)
    lax.fori_loop(1, 4, drain_quad, 0)
    lax.fori_loop(0, 4, drain_scot, 0)
    wait(grad_out, dec_send.at[1])

    @pl.when(quad < quads - 1)
    def _():
        wait(dec_out, dec_send.at[0])

    @pl.when(odd == 1)
    def _():
        wait(keep_used, local_sem.at[2])

        @pl.when(quad == quads - 1)
        def _():
            wait(noise_used, local_sem.at[4])


def body(
    clip_pool,
    sample_ids,
    timesteps,
    noise_draw,
    keep_lists,
    enc_weight,
    enc_gain,
    dec_weight,
    dec_gain,
):
    sections = lax.axis_size("section")
    micros = noise_draw.shape[0]
    channels = noise_draw.shape[-1]
    positions = noise_draw.shape[1] * noise_draw.shape[2] * noise_draw.shape[3]
    scale = 1.0 / math.sqrt(micros * lax.axis_size("dp") * positions)
    lined = (micros, positions, channels)
    noise = noise_draw.reshape(lined)
    clips = clip_pool.reshape((-1,) + lined[1:])
    clean = jnp.zeros(lined, F32)
    for clip in range(clips.shape[0]):
        clean = jnp.where((sample_ids == clip)[:, None, None], clips[clip][None].astype(F32), clean)
    level = noise_level(timesteps)[:, None, None]
    first = (jnp.sqrt(level) * clean + jnp.sqrt(1.0 - level) * noise.astype(F32)).astype(BF16)
    keeps = jnp.broadcast_to(keep_lists.astype(F32)[:, :, None], keep_lists.shape + (128,))
    member = np.arange(channels) // (channels // GROUPS)
    mix = jnp.asarray((member[:, None] == member[None, :]).astype(np.float32), BF16)
    vmem = pl.BlockSpec(memory_space=pltpu.VMEM)
    hbm = pl.BlockSpec(memory_space=pl.ANY)
    slots = lambda *lead: pltpu.VMEM(lead + (positions, channels), BF16)
    kept = lambda *lead: pltpu.VMEM(lead + (3, 8, channels), F32)
    rows = 32 * micros
    group = lax.axis_size("dp")
    chips = group // 2
    wide = lambda *lead: pltpu.VMEM(lead + (40, channels), BF16)
    enc_blocks, dec_blocks = 9 * channels // group // 40, 3 * channels // group // 40
    shares = lambda n: [wide(chips, 2, n), wide(chips, n), wide(chips, n), wide(chips - 1, n)]
    dwe, dwd, gains = pl.pallas_call(
        lambda *refs: pipeline_kernel(sections, micros, scale, *refs),
        out_shape=(
            jax.ShapeDtypeStruct((enc_blocks, 40, channels), F32),
            jax.ShapeDtypeStruct((dec_blocks, 40, channels), F32),
            jax.ShapeDtypeStruct((8, channels), F32),
        ),
        in_specs=[vmem, vmem, vmem, vmem, vmem, vmem, hbm, hbm],
        out_specs=(vmem, vmem, vmem),
        scratch_shapes=[
            pltpu.VMEM((9 * channels, channels), BF16),
            pltpu.VMEM((4, 3 * channels, channels), BF16),
            pltpu.VMEM((micros, 2 * sections, 128), F32),
            slots(micros),
            pltpu.VMEM((4, 8, channels), F32),
            slots(micros),
            slots(micros),
            slots(4, 2),
            slots(micros),
            slots(2),
            slots(2),
            slots(micros),
            slots(2),
            slots(2),
            slots(4, 2),
            slots(micros),
            kept(micros),
            kept(micros),
            pltpu.VMEM((micros, 8, channels), F32),
            pltpu.VMEM((rows, channels), BF16),
            pltpu.VMEM((rows, 9 * channels), BF16),
            kept(4, 2),
            kept(4, 2),
            pltpu.VMEM((4, 2, 8, channels), F32),
            slots(4, 2),
            slots(4, 2),
            pltpu.VMEM((4, 8, channels), F32),
            slots(micros),
            slots(micros),
            pltpu.VMEM((4, 8, channels), F32),
            pltpu.VMEM((rows, channels), BF16),
            pltpu.VMEM((rows, 3 * channels), BF16),
            pltpu.VMEM((64, channels), F32),
            pltpu.VMEM((channels, rows), BF16),
            pltpu.VMEM((8, channels), F32),
            pltpu.VMEM((8, channels), F32),
            pltpu.VMEM((8, channels), F32),
            pltpu.VMEM((8, channels), F32),
            pltpu.VMEM((chips - 1, 8, channels), F32),
            *shares(enc_blocks),
            *shares(dec_blocks),
            pltpu.SemaphoreType.DMA((6,)),
            pltpu.SemaphoreType.DMA((2, 4)),
            pltpu.SemaphoreType.DMA((2, 4)),
            pltpu.SemaphoreType.DMA((4,)),
            pltpu.SemaphoreType.DMA((4,)),
            pltpu.SemaphoreType.DMA((micros,)),
            pltpu.SemaphoreType.DMA((micros + 4,)),
            pltpu.SemaphoreType.DMA((4, 2)),
            pltpu.SemaphoreType.DMA((4,)),
            pltpu.SemaphoreType.DMA((3,)),
            pltpu.SemaphoreType.DMA,
            pltpu.SemaphoreType.DMA((3, 4)),
            pltpu.SemaphoreType.DMA((3, 4)),
            pltpu.SemaphoreType.DMA((3, micros)),
            pltpu.SemaphoreType.DMA((6,)),
            pltpu.SemaphoreType.DMA((2, chips)),
            pltpu.SemaphoreType.DMA((2, 3, chips - 1)),
            pltpu.SemaphoreType.DMA((2, chips)),
            pltpu.SemaphoreType.DMA((2, 3, chips - 1)),
            pltpu.SemaphoreType.DMA((2,)),
            pltpu.SemaphoreType.DMA((2, chips - 1)),
        ],
        compiler_params=pltpu.CompilerParams(
            collective_id=0, has_side_effects=True, vmem_limit_bytes=60 << 20
        ),
        name="pipeline",
    )(keeps, first, noise, enc_gain, dec_gain, mix, enc_weight[0], dec_weight[0])
    part = channels // group
    gains = lax.dynamic_slice_in_dim(gains, lax.axis_index("dp") * part, part, 1)
    return (
        dwe.reshape(1, -1, channels),
        gains[0:1],
        dwd.reshape(1, -1, channels),
        gains[1:2],
    )


def solution(mesh):
    placed = (
        P("dp", None, None, None, None),
        P("dp"),
        P("dp"),
        P("dp", None, None, None, None),
        P("dp", None),
        P("section", None, None),
        P("section", None),
        P("section", None, None),
        P("section", None),
    )
    return jax.shard_map(
        body,
        mesh=mesh,
        in_specs=placed,
        out_specs=(
            P("section", "dp", None),
            P("section", "dp"),
            P("section", "dp", None),
            P("section", "dp"),
        ),
        check_vma=False,
    )
```
